32 devices in a mesh: gx: 16 (over z, y, x), gy: 2 (over core).
Axes of the slice: x: 2, y: 2, z: 4, core: 2. Of those that a mesh axis runs over, the one named last changes fastest.
Arguments:
- background: float32 [27, 16, 32, 256], P(None, None, 'gx', 'gy'), as said below
- overset_block: float32 [27, 16, 16, 256], P(None, None, 'gx', 'gy'), as said below
- solid_mask: int32 [16, 16, 256], P(None, 'gx', 'gy'), may hold values 0 or 1
- donor_tile: int32 [16, 2, 16], P('gx', 'gy'), may hold values from 0 to 31
- target_rank: int32 [16, 2, 16, 1], P('gx', 'gy'), may hold values from 0 to 15; in each aligned block of 16 rows (0 to 15, 16 to 31, ..., all dimensions but the last counted through in order) at most 2 rows name the same one
- target_slot: int32 [16, 2, 16], P('gx', 'gy'), may hold values from 0 to 3
- fringe_tiles: int32 [16, 2, 4], P('gx', 'gy'), may hold values from 0 to 15, as said below
- interp_weights: bfloat16 [16, 2, 16, 128, 128], P('gx', 'gy'), as said below
Outputs:
- background_next: float32 [27, 16, 32, 256], P(None, None, 'gx', 'gy')
- overset_next: float32 [27, 16, 16, 256], P(None, None, 'gx', 'gy')
The draws below stay inside these ranges and needn't reach their ends.
Inputs may be any that keep to these rules, and one draw needn't show every extreme that they name: `background`: positive. `overset_block`: positive. `interp_weights`: nonnegative. `target_rank`: among the 16 jobs of one block no value appears more than 2 times; in some block some value appears exactly 2 times. `fringe_tiles`: the 4 entries of one block are distinct.
All inputs are finite; a program needn't handle non-finite values. No bound on the sum of `solid_mask` on one device may be relied on, other than what follows from the above.
Results may differ from the reference program's by a relative error of at most 0.0012.
Values may be sent and summed in bfloat16 or wider, within the bound.
A program may use at most 64 MiB of HBM per device.

```python
import math
import jax
import jax.numpy as jnp
import numpy as np
from jax import lax

NZ = 16
TILE = 128
CAP = 2
STEPS = 2
BX_DEV = 2
BY_DEV = 128
KX_DEV = 1
KY_DEV = 128
FRINGE = 4
BX = 32
BY = 256
KX = 16
KY = 256
DONOR_TILES = 32
BODY_TILES = 16
JOBS = 16
N_GX = 16
N_GY = 2


def lattice_tables_drawn():
    velocity = []
    weight = []
    for shift_x in (-1, 0, 1):
        for shift_y in (-1, 0, 1):
            for shift_z in (-1, 0, 1):
                speed = abs(shift_x) + abs(shift_y) + abs(shift_z)
                velocity.append((shift_x, shift_y, shift_z))
                weight.append((8.0 / 27.0, 2.0 / 27.0, 1.0 / 54.0, 1.0 / 216.0)[speed])
    return (np.array(velocity, np.float32), np.array(weight, np.float32))


def populations(key, depth, width_x, width_y):
    velocity, weight = lattice_tables_drawn()
    first, second, third, fourth = jax.random.split(key, 4)
    position = jnp.arange(width_x, dtype=jnp.float32) / max(width_x - 1, 1)
    rough = jax.random.uniform(first, (depth, width_x, width_y), jnp.float32, -1.0, 1.0)
    log_scale = jax.random.uniform(fourth, (N_GX, N_GY), jnp.float32, -0.6931472, 0.6931472)
    block_scale = jnp.exp(log_scale)
    block_scale = jnp.repeat(jnp.repeat(block_scale, width_x // N_GX, axis=0), width_y // N_GY, axis=1)
    density = (1.0 + 2.0 * position)[None, :, None] * (1.0 + 0.2 * rough)
    density = density * block_scale[None]
    flow = jax.random.uniform(second, (3, depth, width_x, width_y), jnp.float32, -0.015, 0.015)
    noise = jax.random.uniform(third, (27, depth, width_x, width_y), jnp.float32, -0.8, 0.8)
    along = jnp.einsum('qa,azxy->qzxy', jnp.asarray(velocity), flow)
    return jnp.asarray(weight)[:, None, None, None] * density[None] * (1.0 + 3.0 * along + noise)


def draw_background(key, part):
    return populations(jax.random.fold_in(key, 11), NZ, BX, BY)


def draw_overset_block(key, part):
    return populations(jax.random.fold_in(key, 23), NZ, KX, KY)


def draw_fringe_tiles(key, part):
    scores = jax.random.randint(jax.random.fold_in(key, 37), (N_GX, N_GY, BODY_TILES), 0, 1 << 20)
    scores = scores * BODY_TILES + jnp.arange(BODY_TILES, dtype=jnp.int32)
    order = jnp.argsort(scores, axis=-1, stable=True)
    return order[:, :, :FRINGE].astype(jnp.int32)


def draw_interp_weights(key, part):
    first, second = jax.random.split(jax.random.fold_in(key, 53))
    spread = jax.random.uniform(first, (N_GX, N_GY, JOBS, TILE, TILE), jnp.float32, 0.0, 1.0)
    diagonal = jax.random.uniform(second, (N_GX, N_GY, JOBS, TILE), jnp.float32, 0.5, 1.0)
    off_scale = 0.5
    matrix = off_scale * spread / TILE + diagonal[..., None] * jnp.eye(TILE, dtype=jnp.float32)
    return matrix.astype(jnp.bfloat16)


def plant(values, rng, smallest, largest):
    index_at = [jax.random.randint(jax.random.fold_in(rng, axis), (), 0, length) for axis, length in enumerate(values.shape)]
    main_axis = values.shape.index(max(values.shape))
    neighbour = index_at[:main_axis] + [(index_at[main_axis] + 1) % values.shape[main_axis]] + index_at[main_axis + 1:]
    return values.at[tuple(index_at)].set(smallest).at[tuple(neighbour)].set(largest)


def routed_block(key, own, number, rows, number_of, top, most, slope):
    ranking = jax.random.permutation(key, number_of)
    packed, usual = portions_of(number_of, rows * top, most, slope, True), portions_of(number_of, rows * top, most, slope, False)
    places = jnp.arange(number_of)

    def named(sizes, turn):
        used = int((sizes > 0).sum())
        fixed = max(1, used // 4)
        shifted = fixed + (places - fixed + turn * (used - fixed)) % max(1, number_of - fixed)
        return jnp.zeros((number_of,), jnp.int32).at[ranking[jnp.where(places < fixed, places, shifted)]].set(jnp.asarray(sizes, jnp.int32))

    sizes = jnp.where(number % 4 == 0, named(packed, number // 4), named(usual, number - number // 4 - 1))
    mixed = jax.random.permutation(jax.random.fold_in(own, 3), number_of)
    donor, sink = mixed[0:number_of // 2 * 2:2], mixed[1:number_of // 2 * 2:2]
    margin = jnp.minimum(sizes[donor] - 1, most - sizes[sink]) // 2
    margin = jnp.where((donor == ranking[0]) | (sink == ranking[0]) | (sizes[sink] == 0), 0, jnp.maximum(margin, 0))
    shifted = jax.random.randint(jax.random.fold_in(own, 4), (number_of // 2,), 0, 1 << 20) % (margin + 1)
    sizes = sizes.at[donor].add(-shifted).at[sink].add(shifted)
    items = jnp.searchsorted(jnp.cumsum(sizes), jnp.arange(rows * top), side="right").astype(jnp.int32)
    listing = items.reshape(top, rows).T
    listing = listing[jax.random.permutation(jax.random.fold_in(own, 1), rows)]
    turn = jax.random.randint(jax.random.fold_in(own, 2), (rows, 1), 0, top)
    return jnp.take_along_axis(listing, (jnp.arange(top)[None, :] + turn) % top, axis=1)


def portions_of(amount, total, limit, slope, full):
    portions = [(1 << 20) // math.isqrt(standing ** slope) + 1 for standing in range(1, amount + 1)]
    largest = limit if full else min(limit, max(-(-total // amount), total * portions[0] // sum(portions)))
    least = 1 if total - largest >= amount - 1 else 0
    given, rest = [largest] + [least] * (amount - 1), total - largest - least * (amount - 1)
    while rest > 0:
        free = [i for i in range(1, amount) if given[i] < largest] or [i for i in range(1, amount) if given[i] < limit]
        pool, remaining = sum([portions[i] for i in free]), rest
        for i in free:
            addition = min(limit - given[i], max(1, remaining * portions[i] // pool), rest)
            given[i] = given[i] + addition
            rest = rest - addition
    return np.array(given)


def setup_inputs(seed: int = 0) -> dict:
    key_list = jax.random.split(jax.random.key(seed), 9)
    background = draw_background(jax.random.fold_in(key_list[8], 71), 0)
    overset_block = draw_overset_block(jax.random.fold_in(key_list[8], 71), 0)
    solid_mask = plant((jax.random.randint(key_list[2], (NZ, KX, KY), 0, 8) < 1).astype(jnp.int32), jax.random.fold_in(key_list[2], 1), 0, 1)
    donor_tile = plant(jax.random.randint(key_list[3], (N_GX, N_GY, JOBS), 0, DONOR_TILES), jax.random.fold_in(key_list[3], 1), 0, DONOR_TILES - 1).astype(jnp.int32)
    target_rank_keys = jax.random.split(jax.random.fold_in(key_list[4], 1), N_GX * N_GY * JOBS // JOBS)
    target_rank_turns = jax.random.permutation(jax.random.fold_in(key_list[4], 3), N_GX * N_GY * JOBS // JOBS)
    target_rank = jax.vmap(lambda own, number: routed_block(jax.random.fold_in(key_list[4], 2), own, number, JOBS, N_GX, 1, CAP, 2))(target_rank_keys, target_rank_turns).reshape((N_GX, N_GY, JOBS, 1))
    target_slot = plant(jax.random.randint(key_list[5], (N_GX, N_GY, JOBS), 0, FRINGE), jax.random.fold_in(key_list[5], 1), 0, FRINGE - 1).astype(jnp.int32)
    fringe_tiles = draw_fringe_tiles(jax.random.fold_in(key_list[8], 71), 0)
    interp_weights = draw_interp_weights(jax.random.fold_in(key_list[8], 71), 0)
    return {"background": background, "overset_block": overset_block, "solid_mask": solid_mask, "donor_tile": donor_tile, "target_rank": target_rank, "target_slot": target_slot, "fringe_tiles": fringe_tiles, "interp_weights": interp_weights}


RELAXATION = 1.25


def lattice_tables():
    velocity = []
    weight = []
    for shift_x in (-1, 0, 1):
        for shift_y in (-1, 0, 1):
            for shift_z in (-1, 0, 1):
                speed = abs(shift_x) + abs(shift_y) + abs(shift_z)
                velocity.append((shift_x, shift_y, shift_z))
                weight.append((8.0 / 27.0, 2.0 / 27.0, 1.0 / 54.0, 1.0 / 216.0)[speed])
    return np.array(velocity), np.array(weight)


def stream_global(fields):
    velocity, weight = lattice_tables()
    parts = []
    for direction in range(27):
        shift_x, shift_y, shift_z = [int(component) for component in velocity[direction]]
        parts.append(jnp.roll(fields[direction], (shift_z, shift_x, shift_y), axis=(0, 1, 2)))
    return jnp.stack(parts)


def collide(fields, solid_cells=None):
    velocity, weight = lattice_tables()
    vectors = jnp.asarray(velocity.astype(np.float32))
    weights_q = jnp.asarray(weight.astype(np.float32))
    density = jnp.sum(fields, axis=0)
    moment = jnp.einsum('qa,qzxy->azxy', vectors, fields, precision=lax.Precision.HIGHEST)
    flow = moment / density
    along = jnp.einsum('qa,azxy->qzxy', vectors, flow, precision=lax.Precision.HIGHEST)
    square = jnp.sum(flow * flow, axis=0)
    equilibrium = weights_q[:, None, None, None] * density * (1.0 + 3.0 * along + 4.5 * along * along - 1.5 * square)
    relaxed = fields - RELAXATION * (fields - equilibrium)
    if solid_cells is not None:
        relaxed = jnp.where(solid_cells[None] == 1, fields[::-1], relaxed)
    return relaxed


def to_tiles(fields, width_x, width_y):
    depth = fields.shape[1]
    shaped = fields.reshape(27, depth, N_GX, width_x, N_GY, width_y // TILE, TILE)
    shaped = jnp.transpose(shaped, (2, 4, 0, 1, 3, 5, 6))
    return shaped.reshape(N_GX, N_GY, 27, depth * width_x * (width_y // TILE), TILE)


def from_tiles(tiles, depth, width_x, width_y):
    shaped = tiles.reshape(N_GX, N_GY, 27, depth, width_x, width_y // TILE, TILE)
    shaped = jnp.transpose(shaped, (2, 3, 0, 4, 1, 5, 6))
    return shaped.reshape(27, depth, N_GX * width_x, N_GY * width_y)


def reference(background, overset_block, solid_mask, donor_tile, target_rank, target_slot, fringe_tiles, interp_weights):
    current_bg = background
    current_body = overset_block
    for step in range(STEPS):
        bg_read = stream_global(current_bg)
        body_read = stream_global(current_body)
        bg_tiles = to_tiles(bg_read, BX_DEV, BY_DEV)

        def accumulate(owner, gathered):
            source = bg_tiles[owner]
            picked = jnp.take_along_axis(source, donor_tile[owner][:, None, :, None], axis=2)
            blocks = interp_weights[owner].astype(jnp.float32)
            contribution = jnp.einsum('hqjm,hjmn->hjqn', picked, blocks, precision=lax.Precision.HIGHEST)
            layer = jnp.broadcast_to(jnp.arange(N_GY, dtype=jnp.int32)[:, None], target_slot[owner].shape)
            return gathered.at[target_rank[owner, :, :, 0], layer, target_slot[owner]].add(contribution)

        interp = lax.fori_loop(0, N_GX, accumulate, jnp.zeros((N_GX, N_GY, FRINGE, 27, TILE), jnp.float32))
        interp = jnp.transpose(interp, (0, 1, 3, 2, 4))
        body_tiles = to_tiles(body_read, KX_DEV, KY_DEV)
        fringe_old = jnp.take_along_axis(body_tiles, fringe_tiles[:, :, None, :, None], axis=3)
        mass_target = jnp.sum(fringe_old)
        mass_interp = jnp.sum(interp)
        fringe_new = 0.5 * (fringe_old + (mass_target / mass_interp) * interp)
        selector = (fringe_tiles[:, :, :, None] == jnp.arange(BODY_TILES, dtype=jnp.int32)).astype(jnp.float32)
        covered = jnp.sum(selector, axis=2) > 0
        placed = jnp.einsum('ghrk,ghqrn->ghqkn', selector, fringe_new, precision=lax.Precision.HIGHEST)
        mixed_tiles = jnp.where(covered[:, :, None, :, None], placed, body_tiles)
        body_mixed = from_tiles(mixed_tiles, NZ, KX_DEV, KY_DEV)
        current_bg = collide(bg_read)
        current_body = collide(body_mixed, solid_mask)
    return current_bg, current_body
```

```python
import functools

import jax
import jax.numpy as jnp
import numpy as np
from jax import lax
from jax.experimental import pallas as pl
from jax.experimental.pallas import tpu as pltpu
from jax.sharding import PartitionSpec as P

CAP = 2
STEPS = 2
RELAXATION = 1.25
ROWS = 32
MESH = pl.DeviceIdType.MESH

VELOCITY = [(x, y, z) for x in (-1, 0, 1) for y in (-1, 0, 1) for z in (-1, 0, 1)]
WEIGHT = [(8 / 27, 2 / 27, 1 / 54, 1 / 216)[abs(x) + abs(y) + abs(z)] for x, y, z in VELOCITY]

RIGHT, LEFT, ACROSS, ACROSS_RIGHT, ACROSS_LEFT = range(5)


def column_lists(width):
    lists = {ACROSS: [], ACROSS_RIGHT: [], ACROSS_LEFT: []}
    for q, (cx, cy, _) in enumerate(VELOCITY):
        if cy == 0:
            continue
        for x in range(width):
            to = x + cx
            way = ACROSS_RIGHT if to >= width else ACROSS_LEFT if to < 0 else ACROSS
            lists[way].append((q, x))
    return lists


def pack_columns(plane, columns, lanes, length):
    packed = jnp.zeros(lanes.shape, jnp.float32)
    for k, (q, x) in enumerate(columns):
        edge = length - 1 if VELOCITY[q][1] == 1 else 0
        value = plane(q, x)
        if (k - edge) % length:
            value = pltpu.roll(value, (k - edge) % length, 1)
        packed = jnp.where(lanes == k, value, packed)
    return packed


def stream(plane, across_x, packs, width, lanes, depth, length, store):
    lists = column_lists(width)
    where_is = {way: {c: k for k, c in enumerate(cols)} for way, cols in lists.items()}
    for q, (cx, cy, cz) in enumerate(VELOCITY):
        for x in range(width):
            source = x - cx
            if source < 0:
                value, way, column = across_x(RIGHT, q - 18), ACROSS_RIGHT, (q, width - 1)
            elif source >= width:
                value, way, column = across_x(LEFT, q), ACROSS_LEFT, (q, 0)
            else:
                value, way, column = plane(q, source), ACROSS, (q, source)
            if cy:
                edge = 0 if cy == 1 else length - 1
                k = where_is[way][column]
                outer = packs(way)
                if (edge - k) % length:
                    outer = pltpu.roll(outer, (edge - k) % length, 1)
                value = jnp.where(lanes == edge, outer, pltpu.roll(value, cy % length, 1))
            if cz:
                value = pltpu.roll(value, cz % depth, 0)
            store(q, x, value)


def collide(load, store, solid=None):
    density = None
    moment = [None, None, None]
    for q, velocity in enumerate(VELOCITY):
        value = load(q)
        density = value if density is None else density + value
        for axis in range(3):
            if velocity[axis]:
                signed = value if velocity[axis] == 1 else -value
                moment[axis] = signed if moment[axis] is None else moment[axis] + signed
    flow = [m / density for m in moment]
    square = flow[0] * flow[0] + flow[1] * flow[1] + flow[2] * flow[2]
    base = 1.0 - 1.5 * square
    scaled = {w: (RELAXATION * w) * density for w in sorted(set(WEIGHT))}
    for q in range(14):
        along = None
        for axis in range(3):
            if VELOCITY[q][axis]:
                term = flow[axis] if VELOCITY[q][axis] == 1 else -flow[axis]
                along = term if along is None else along + term
        if along is None:
            pairs = [(q, scaled[WEIGHT[q]] * base)]
        else:
            even = scaled[WEIGHT[q]] * (base + 4.5 * along * along)
            odd = scaled[WEIGHT[q]] * (3.0 * along)
            pairs = [(q, even + odd), (26 - q, even - odd)]
        values = [load(p) for p, _ in pairs]
        for (p, equilibrium), value, other in zip(pairs, values, values[::-1]):
            relaxed = (1.0 - RELAXATION) * value + equilibrium
            if solid is not None:
                relaxed = jnp.where(solid, other, relaxed)
            store(p, relaxed)


def kernel(
    groups, layers, fringe_count, *refs,
):
    operands, (out_bg, out_body), loaded, load_sem, *scratch = (
        refs[:8], refs[8:10], refs[10:18], *refs[18:]
    )
    loads = [
        pltpu.make_async_copy(a, b, load_sem.at[i]) for i, (a, b) in enumerate(zip(operands, loaded))
    ]
    for copy in loads:
        copy.start()
    steps(groups, layers, fringe_count, loads, *loaded, out_bg, out_body, *scratch)


def steps(
    groups, layers, fringe_count, loads, donor, target, slot, fringe,
    bg, body, solid, weights, out_bg, out_body,
    bgx_send, bgx_recv, bdx_recv, pk_send, pk_recv, mk_send, mk_recv,
    cur_bg, cur_body, rd_bg, rd_body, contrib, outgoing, arrived,
    sum_send, sum_recv, interp, chosen, label,
    halo_s, halo_r, mask_s, mask_r, a2a_s, a2a_r, tot_s, tot_r,
):
    gx, gy = lax.axis_index("gx"), lax.axis_index("gy")
    devices = groups * layers
    me = gx * layers + gy
    jobs = weights.shape[0]
    depth, length = cur_body.shape[1], cur_body.shape[2]
    width = cur_bg.shape[1]
    right = lax.rem(gx + 1, groups)
    left = lax.rem(gx + groups - 1, groups)
    other = lax.rem(gy + 1, layers)
    peer = [(right, gy), (left, gy), (gx, other), (right, other), (left, other)]

    barrier = pltpu.get_barrier_semaphore()

    def greet(k, carry):
        d = lax.rem(me + k, devices)
        pl.semaphore_signal(
            barrier, inc=1, device_id=(lax.div(d, layers), lax.rem(d, layers)), device_id_type=MESH
        )
        return carry

    lax.fori_loop(1, devices, greet, 0)

    lanes = lax.broadcasted_iota(jnp.int32, (depth, length), 1)
    rows = lax.broadcasted_iota(jnp.int32, (depth, length), 0)
    message_rows = lax.broadcasted_iota(jnp.int32, (ROWS, length), 0)
    bg_columns = column_lists(width)
    body_columns = column_lists(1)
    ways = (ACROSS, ACROSS_RIGHT, ACROSS_LEFT)

    def remote(src, dst, send, recv, to):
        return pltpu.make_async_remote_copy(
            src_ref=src, dst_ref=dst, send_sem=send, recv_sem=recv, device_id=to, device_id_type=MESH
        )

    def bg_halo(step):
        copies = [
            remote(bgx_send.at[step, w], bgx_recv.at[step, w], halo_s.at[step, w],
                   halo_r.at[step, w], peer[w])
            for w in (RIGHT, LEFT)
        ]
        return copies + [
            remote(pk_send.at[step, 0, w - 2], pk_recv.at[step, 0, w - 2], halo_s.at[step, w],
                   halo_r.at[step, w], peer[w])
            for w in ways
        ]

    def body_halo(step):
        source = body if step == 0 else cur_body
        copies = [
            remote(source.at[pl.ds(18 if w == RIGHT else 0, 9)], bdx_recv.at[step, w],
                   halo_s.at[step, 5 + w], halo_r.at[step, 5 + w], peer[w])
            for w in (RIGHT, LEFT)
        ]
        return copies + [
            remote(pk_send.at[step, 1, w - 2], pk_recv.at[step, 1, w - 2], halo_s.at[step, 5 + w],
                   halo_r.at[step, 5 + w], peer[w])
            for w in ways
        ]

    def prepare_bg(step):
        for k in range(9):
            bgx_send[step, RIGHT, k] = cur_bg[18 + k, width - 1].astype(jnp.bfloat16)
            bgx_send[step, LEFT, k] = cur_bg[k, 0].astype(jnp.bfloat16)
        for w in ways:
            pk_send[step, 0, w - 2] = pack_columns(
                lambda q, x: cur_bg[q, x], bg_columns[w], lanes, length
            )

    def prepare_body(step):
        source = body if step == 0 else cur_body
        for w in ways:
            pk_send[step, 1, w - 2] = pack_columns(
                lambda q, x: source[q], body_columns[w], lanes, length
            )

    def stream_bg(step):
        def store(q, x, value):
            rd_bg[pl.ds((q * width + x) * depth, depth), :] = value

        stream(
            lambda q, x: cur_bg[q, x],
            lambda w, k: bgx_recv[step, w, k].astype(jnp.float32),
            lambda w: pk_recv[step, 0, w - 2],
            width, lanes, depth, length, store,
        )

    def stream_body(step):
        source = body if step == 0 else cur_body

        def store(q, x, value):
            rd_body[q] = value

        stream(
            lambda q, x: source[q],
            lambda w, k: bdx_recv[step, w, k],
            lambda w: pk_recv[step, 1, w - 2],
            1, lanes, depth, length, store,
        )

    def collide_bg(last):
        for x in range(width):
            def store(q, value):
                if last:
                    out_bg[q, pl.ds(x, depth, stride=width), :] = value
                else:
                    cur_bg[q, x] = value

            collide(lambda q: rd_bg[pl.ds((q * width + x) * depth, depth), :], store)

    group = next(g for g in (8, 4, 2, 1) if jobs % g == 0)

    def contributions():
        def some(i, total):
            for k in range(group):
                j = i * group + k
                d = donor[j]
                first = lax.rem(d, width) * depth + lax.div(d, width)
                picked = rd_bg[pl.ds(first, ROWS, stride=width * depth), :]
                high = picked.astype(jnp.bfloat16)
                low = (picked - high.astype(jnp.float32)).astype(jnp.bfloat16)
                both = jnp.concatenate([high, low], axis=0)
                product = jnp.dot(both, weights[j], preferred_element_type=jnp.float32)
                product = product[:ROWS] + product[ROWS:]
                contrib[j] = product
                total = total + product
            return total

        total = lax.fori_loop(0, jobs // group, some, jnp.zeros((ROWS, length), jnp.float32))
        return jnp.sum(total, axis=0, keepdims=True)

    def message(d, c):
        value = contrib[chosen[d * CAP + c]]
        entry = jnp.full((ROWS, length), label[d * CAP + c], jnp.int32).astype(jnp.float32)
        return jnp.where(message_rows == 27, entry, value).astype(jnp.bfloat16)

    def send_contributions(step):
        def to(k, carry):
            d = lax.rem(gx + 1 + lax.rem(k - 1 + groups // 2 - 1, groups - 1), groups)
            for c in range(CAP):
                outgoing[step, d, pl.ds(c * ROWS, ROWS), :] = message(d, c)
            remote(outgoing.at[step, d], arrived.at[step, gx], a2a_s.at[step], a2a_r.at[step],
                   (d, gy)).start()
            return carry

        lax.fori_loop(1, groups, to, 0)
        for c in range(CAP):
            arrived[step, gx, pl.ds(c * ROWS, ROWS), :] = message(gx, c)

    def wait_bytes(ref, semaphore):
        pltpu.make_async_copy(ref, ref, semaphore).wait()

    def send_sums(step, mass_target, mass_interp):
        both = jnp.concatenate([mass_target, mass_interp], axis=0)
        sum_send[step] = both
        sum_recv[step, me] = both

        def to(k, carry):
            d = lax.rem(me + k, devices)
            remote(sum_send.at[step], sum_recv.at[step, me], tot_s.at[step], tot_r.at[step],
                   (lax.div(d, layers), lax.rem(d, layers))).start()
            return carry

        lax.fori_loop(1, devices, to, 0)

    for copy in loads[:7]:
        copy.wait()
    hits = [rows == fringe[r] for r in range(fringe_count)]
    covered = functools.reduce(jnp.logical_or, hits)

    def mix(step):
        wait_bytes(arrived.at[step, pl.ds(0, groups - 1)], a2a_r.at[step])

        def gather(o, totals):
            for c in range(CAP):
                value = arrived[step, o, pl.ds(c * ROWS, ROWS), :].astype(jnp.float32)
                entry = value[27:28]
                totals = tuple(
                    t + jnp.where(entry == float(r), value, 0.0) for r, t in enumerate(totals)
                )
            return totals

        zero = jnp.zeros((ROWS, length), jnp.float32)
        totals = lax.fori_loop(0, groups, gather, (zero,) * fringe_count)
        for r in range(fringe_count):
            interp[r] = totals[r]
        wait_bytes(sum_recv.at[step, pl.ds(0, devices - 1)], tot_r.at[step])
        sums = jnp.sum(jnp.sum(sum_recv[step], axis=0), axis=1, keepdims=True)
        factor = sums[0:1] / sums[1:2]
        for q in range(27):
            old = rd_body[q]
            fresh = jnp.zeros((depth, length), jnp.float32)
            for r in range(fringe_count):
                fresh = jnp.where(hits[r], interp[r, q : q + 1, :], fresh)
            rd_body[q] = jnp.where(covered, 0.5 * (old + factor * fresh), old)

    for q in range(27):
        for x in range(width):
            cur_bg[q, x] = bg[q, pl.ds(x, depth, stride=width), :]
    prepare_bg(0)
    prepare_body(0)
    mine = covered.astype(jnp.float32)
    mk_send[...] = mine
    masks = [
        remote(mk_send, mk_recv.at[w], mask_s.at[w], mask_r.at[w], peer[w]) for w in range(5)
    ]
    rd_bg[pl.ds(27 * width * depth, (ROWS - 27) * width * depth), :] = jnp.zeros(
        ((ROWS - 27) * width * depth, length), jnp.float32
    )
    contrib[jobs] = jnp.zeros((ROWS, length), jnp.float32)

    pl.semaphore_wait(barrier, devices - 1)
    bg_copies = [bg_halo(step) for step in range(STEPS)]
    body_copies = [body_halo(step) for step in range(STEPS)]
    for copy in bg_copies[0] + body_copies[0] + masks:
        copy.start()

    def choose(d, carry):
        def scan(i, found):
            first, second = found
            j = jobs - 1 - i
            match = target[j] == d
            second = jnp.where(match, first, second)
            first = jnp.where(match, j, first)
            return first, second

        found = lax.fori_loop(0, jobs, scan, (jnp.int32(jobs), jnp.int32(jobs)))
        for c in range(CAP):
            chosen[d * CAP + c] = found[c]
            held = slot[jnp.minimum(found[c], jobs - 1)]
            label[d * CAP + c] = jnp.where(found[c] < jobs, held, -1)
        return carry

    lax.fori_loop(0, groups, choose, 0)

    for copy in bg_copies[0]:
        copy.wait_recv()
    stream_bg(0)
    collide_bg(False)
    prepare_bg(1)
    for copy in bg_copies[1]:
        copy.start()
    loads[7].wait()
    mass_interp = contributions()
    send_contributions(0)
    for copy in body_copies[0]:
        copy.wait_recv()
    stream_body(0)
    held = jnp.zeros((depth, length), jnp.float32)
    for q in range(27):
        held = held + rd_body[q]
    held = jnp.where(covered, held, 0.0)
    send_sums(0, jnp.sum(held, axis=0, keepdims=True), mass_interp)

    for copy in bg_copies[1]:
        copy.wait_recv()
    stream_bg(1)
    mass_interp = contributions()
    send_contributions(1)

    mix(0)
    is_solid = solid[...] == 1

    def store_body(q, value):
        cur_body[q] = value

    collide(lambda q: rd_body[q], store_body, is_solid)
    prepare_body(1)
    for copy in body_copies[1]:
        copy.start()
    for copy in masks:
        copy.wait_recv()
    ahead = {0: (mine, mk_recv[ACROSS]), 1: (mk_recv[LEFT], mk_recv[ACROSS_LEFT]),
             -1: (mk_recv[RIGHT], mk_recv[ACROSS_RIGHT])}
    held = jnp.zeros((depth, length), jnp.float32)
    for q, (cx, cy, cz) in enumerate(VELOCITY):
        near, far = ahead[cx]
        share = near
        if cy:
            share = jnp.where(lanes == (length - 1 if cy == 1 else 0), far, near)
        if cz:
            share = pltpu.roll(share, (-cz) % depth, 0)
        held = held + share * cur_body[q]
    send_sums(1, jnp.sum(held, axis=0, keepdims=True), mass_interp)

    collide_bg(True)
    for copy in body_copies[1]:
        copy.wait_recv()
    stream_body(1)
    mix(1)

    def store_out(q, value):
        out_body[q] = value

    collide(lambda q: rd_body[q], store_out, is_solid)

    for copy in masks:
        copy.wait_send()
    for step in range(STEPS):
        for copy in bg_copies[step] + body_copies[step]:
            copy.wait_send()
        wait_bytes(outgoing.at[step, pl.ds(0, groups - 1)], a2a_s.at[step])
        wait_bytes(sum_recv.at[step, pl.ds(0, devices - 1)], tot_s.at[step])


def hand_over(bg, body, out_bg, out_body, store_sem):
    stores = []
    for source, out in ((bg, out_bg), (body, out_body)):
        for k in range(3):
            span = pl.ds(9 * k, 9)
            stores.append(pltpu.make_async_copy(source.at[span], out.at[span], store_sem.at[len(stores)]))
    for store in stores:
        store.start()
    for store in stores:
        store.wait()


def local(groups, layers, background, overset_block, solid_mask, donor_tile, target_rank,
          target_slot, fringe_tiles, interp_weights):
    _, depth, width, length = background.shape
    jobs, nodes = interp_weights.shape[2], interp_weights.shape[3]
    assert overset_block.shape[2] == 1 and nodes == length and layers == 2 and STEPS == 2
    fringe_count = fringe_tiles.shape[-1]
    devices = groups * layers
    plane = (depth, length)
    f32, bf16 = jnp.float32, jnp.bfloat16
    vmem, smem = pltpu.VMEM, pltpu.SMEM
    dma = pltpu.SemaphoreType.DMA
    next_bg, next_body = pl.pallas_call(
        functools.partial(kernel, groups, layers, fringe_count),
        out_shape=(
            vmem((27, depth * width, length), f32),
            vmem((27, depth, length), f32),
        ),
        in_specs=[pl.BlockSpec(memory_space=pltpu.HBM)] * 8,
        out_specs=(pl.BlockSpec(memory_space=pltpu.VMEM),) * 2,
        scratch_shapes=[
            smem((jobs,), jnp.int32),
            smem((jobs,), jnp.int32),
            smem((jobs,), jnp.int32),
            smem((fringe_count,), jnp.int32),
            vmem((27, depth * width, length), f32),
            vmem((27, depth, length), f32),
            vmem((depth, length), jnp.int32),
            vmem((jobs, nodes, nodes), bf16),
            dma((8,)),
            vmem((STEPS, 2, 9) + plane, bf16),
            vmem((STEPS, 2, 9) + plane, bf16),
            vmem((STEPS, 2, 9) + plane, f32),
            vmem((STEPS, 2, 3) + plane, f32),
            vmem((STEPS, 2, 3) + plane, f32),
            vmem(plane, f32),
            vmem((5,) + plane, f32),
            vmem((27, width) + plane, f32),
            vmem((27,) + plane, f32),
            vmem((ROWS * width * depth, length), f32),
            vmem((27,) + plane, f32),
            vmem((jobs + 1, ROWS, length), f32),
            vmem((STEPS, groups, CAP * ROWS, length), bf16),
            vmem((STEPS, groups, CAP * ROWS, length), bf16),
            vmem((STEPS, 2, length), f32),
            vmem((STEPS, devices, 2, length), f32),
            vmem((fringe_count, ROWS, length), f32),
            smem((groups * CAP,), jnp.int32),
            smem((groups * CAP,), jnp.int32),
            dma((STEPS, 10)),
            dma((STEPS, 10)),
            dma((5,)),
            dma((5,)),
            dma((STEPS,)),
            dma((STEPS,)),
            dma((STEPS,)),
            dma((STEPS,)),
        ],
        compiler_params=pltpu.CompilerParams(
            collective_id=0, has_side_effects=True, vmem_limit_bytes=48000000
        ),
    )(*(pltpu.with_memory_space_constraint(a, pltpu.HBM) for a in (
        donor_tile.reshape(jobs),
        target_rank.reshape(jobs),
        target_slot.reshape(jobs),
        fringe_tiles.reshape(fringe_count),
        background.reshape(27, depth * width, length),
        overset_block.reshape(27, depth, length),
        solid_mask.reshape(depth, length),
        interp_weights.reshape(jobs, nodes, nodes),
    )))
    shapes = (
        jax.ShapeDtypeStruct(next_bg.shape, f32),
        jax.ShapeDtypeStruct(next_body.shape, f32),
    )
    next_bg, next_body = pl.pallas_call(
        hand_over,
        out_shape=shapes,
        in_specs=[pl.BlockSpec(memory_space=pltpu.VMEM)] * 2,
        out_specs=(pl.BlockSpec(memory_space=pltpu.HBM),) * 2,
        scratch_shapes=[dma((6,))],
    )(*(pltpu.with_memory_space_constraint(a, pltpu.VMEM) for a in (next_bg, next_body)))
    return next_bg.reshape(background.shape), next_body.reshape(overset_block.shape)


def solution(mesh):
    return jax.shard_map(
        functools.partial(local, mesh.shape["gx"], mesh.shape["gy"]),
        mesh=mesh,
        in_specs=(
            P(None, None, "gx", "gy"),
            P(None, None, "gx", "gy"),
            P(None, "gx", "gy"),
            P("gx", "gy", None),
            P("gx", "gy", None, None),
            P("gx", "gy", None),
            P("gx", "gy", None),
            P("gx", "gy", None, None, None),
        ),
        out_specs=(P(None, None, "gx", "gy"), P(None, None, "gx", "gy")),
        check_vma=False,
    )
```

```python
import functools

import jax
import jax.numpy as jnp
import numpy as np
from jax import lax
from jax.experimental import pallas as pl
from jax.experimental.pallas import tpu as pltpu
from jax.sharding import PartitionSpec as P

CAP = 2
STEPS = 2
RELAXATION = 1.25
HALF = 16
EARLY = 15
MESH = pl.DeviceIdType.MESH

VELOCITY = [(x, y, z) for x in (-1, 0, 1) for y in (-1, 0, 1) for z in (-1, 0, 1)]
WEIGHT = [(8 / 27, 2 / 27, 1 / 54, 1 / 216)[abs(x) + abs(y) + abs(z)] for x, y, z in VELOCITY]

RIGHT, LEFT, ACROSS, ACROSS_RIGHT, ACROSS_LEFT = range(5)


def column_lists(width):
    lists = {ACROSS: [], ACROSS_RIGHT: [], ACROSS_LEFT: []}
    for q, (cx, cy, _) in enumerate(VELOCITY):
        if cy == 0:
            continue
        for x in range(width):
            to = x + cx
            way = ACROSS_RIGHT if to >= width else ACROSS_LEFT if to < 0 else ACROSS
            lists[way].append((q, x))
    return lists


def unrolled(start, stop, body):
    step = next(n for n in (16, 8, 4, 2, 1) if (stop - start) // n >= 1)

    def several(i, carry):
        for k in range(step):
            body(start + i * step + k, 0)
        return carry

    whole = (stop - start) // step
    lax.fori_loop(0, whole, several, 0)
    for k in range(start + whole * step, stop):
        body(k, 0)


def pack_columns(packed, plane, columns, first, lanes, length):
    for k, (q, x) in enumerate(columns, first):
        edge = length - 1 if VELOCITY[q][1] == 1 else 0
        value = plane(q, x)
        if (k - edge) % length:
            value = pltpu.roll(value, (k - edge) % length, 1)
        packed = jnp.where(lanes == k, value, packed)
    return packed


def stream(plane, across_x, packs, first, width, lanes, depth, length, store, inner=True, outer=True):
    lists = column_lists(width)
    where_is = {way: {c: k for k, c in enumerate(cols, first[way])} for way, cols in lists.items()}
    for q, (cx, cy, cz) in enumerate(VELOCITY):
        for x in range(width):
            source = x - cx
            if not (inner if 0 <= source < width else outer):
                continue
            if source < 0:
                value, way, column = across_x(RIGHT, q - 18), ACROSS_RIGHT, (q, width - 1)
            elif source >= width:
                value, way, column = across_x(LEFT, q), ACROSS_LEFT, (q, 0)
            else:
                value, way, column = plane(q, source), ACROSS, (q, source)
            if cy:
                edge = 0 if cy == 1 else length - 1
                k = where_is[way][column]
                far = packs(way)
                if (edge - k) % length:
                    far = pltpu.roll(far, (edge - k) % length, 1)
                value = jnp.where(lanes == edge, far, pltpu.roll(value, cy % length, 1))
            if cz:
                value = pltpu.roll(value, cz % depth, 0)
            store(q, x, value)


def collide(load, store, solid=None):
    density = None
    moment = [None, None, None]
    for q, velocity in enumerate(VELOCITY):
        value = load(q)
        density = value if density is None else density + value
        for axis in range(3):
            if velocity[axis]:
                signed = value if velocity[axis] == 1 else -value
                moment[axis] = signed if moment[axis] is None else moment[axis] + signed
    flow = [m / density for m in moment]
    square = flow[0] * flow[0] + flow[1] * flow[1] + flow[2] * flow[2]
    base = 1.0 - 1.5 * square
    scaled = {w: (RELAXATION * w) * density for w in sorted(set(WEIGHT))}
    for q in range(14):
        along = None
        for axis in range(3):
            if VELOCITY[q][axis]:
                term = flow[axis] if VELOCITY[q][axis] == 1 else -flow[axis]
                along = term if along is None else along + term
        if along is None:
            pairs = [(q, scaled[WEIGHT[q]] * base)]
        else:
            even = scaled[WEIGHT[q]] * (base + 4.5 * along * along)
            odd = scaled[WEIGHT[q]] * (3.0 * along)
            pairs = [(q, even + odd), (26 - q, even - odd)]
        values = [load(p) for p, _ in pairs]
        for (p, equilibrium), value, other in zip(pairs, values, values[::-1]):
            relaxed = (1.0 - RELAXATION) * value + equilibrium
            if solid is not None:
                relaxed = jnp.where(solid, other, relaxed)
            store(p, relaxed)


def kernel(
    groups, layers, fringe_count, *refs,
):
    operands, (out_bg, out_body), loaded, load_sem, *scratch = (
        refs[:8], refs[8:10], refs[10:18], *refs[18:]
    )
    loads = [
        pltpu.make_async_copy(a, b, load_sem.at[i]) for i, (a, b) in enumerate(zip(operands, loaded))
    ]
    for copy in loads:
        copy.start()
    steps(groups, layers, fringe_count, loads, *loaded, out_bg, out_body, *scratch)


def steps(
    groups, layers, fringe_count, loads, donor, target, slot, fringe,
    bg, body, solid, weights, out_bg, out_body,
    bgx_send, bgx_recv, bdx_send, bdx_recv, pk_send, pk_recv,
    cur_bg, cur_body, rd_bg, rd_body, contrib, outgoing, arrived,
    sum_send, sum_recv, interp, chosen, label,
    halo_s, halo_r, a2a_s, a2a_r, tot_s, tot_r,
):
    gx, gy = lax.axis_index("gx"), lax.axis_index("gy")
    devices = groups * layers
    me = gx * layers + gy
    jobs = weights.shape[0]
    depth, length = cur_body.shape[1], cur_body.shape[2]
    width = cur_bg.shape[1]
    right = lax.rem(gx + 1, groups)
    left = lax.rem(gx + groups - 1, groups)
    other = lax.rem(gy + 1, layers)
    peer = [(right, gy), (left, gy), (gx, other), (right, other), (left, other)]
    f32, bf16 = jnp.float32, jnp.bfloat16

    barrier = pltpu.get_barrier_semaphore()

    def greet(k, carry):
        d = lax.rem(me + k, devices)
        pl.semaphore_signal(
            barrier, inc=1, device_id=(lax.div(d, layers), lax.rem(d, layers)), device_id_type=MESH
        )
        return carry

    with jax.named_scope("greet"):
        unrolled(1, devices, greet)

    lanes = lax.broadcasted_iota(jnp.int32, (depth, length), 1)
    rows = lax.broadcasted_iota(jnp.int32, (depth, length), 0)
    message_rows = lax.broadcasted_iota(jnp.int32, (HALF, length), 0)
    bg_columns = column_lists(width)
    body_columns = column_lists(1)
    ways = (ACROSS, ACROSS_RIGHT, ACROSS_LEFT)
    bg_first = {w: 0 for w in ways}
    body_first = {w: len(bg_columns[w]) for w in ways}
    blank = jnp.zeros((depth, length), f32)

    def remote(src, dst, send, recv, to):
        return pltpu.make_async_remote_copy(
            src_ref=src, dst_ref=dst, send_sem=send, recv_sem=recv, device_id=to, device_id_type=MESH
        )

    def pack_copies(i, at):
        return [
            remote(pk_send.at[i, w - 2], pk_recv.at[i, w - 2], halo_s.at[at + w - 2],
                   halo_r.at[at + w - 2], peer[w])
            for w in ways
        ]

    def x_copies(send, recv, step, planes, at):
        return [
            remote(send.at[step, w, pl.ds(0, planes)], recv.at[step, w, pl.ds(0, planes)],
                   halo_s.at[at + w], halo_r.at[at + w], peer[w])
            for w in (RIGHT, LEFT)
        ]

    packs = [pack_copies(i, 3 * i) for i in range(3)]
    bg_x = [x_copies(bgx_send, bgx_recv, step, 10 - step, 9 + 2 * step) for step in range(STEPS)]
    body_x = [x_copies(bdx_send, bdx_recv, step, 9, 13 + 2 * step) for step in range(STEPS)]

    def pack_bg(w):
        return pack_columns(blank, lambda q, x: cur_bg[q, x], bg_columns[w], bg_first[w], lanes, length)

    def pack_body(packed, source, w):
        return pack_columns(packed, lambda q, x: source[q], body_columns[w], body_first[w], lanes, length)

    def prepare_bg_x(step):
        for k in range(9):
            bgx_send[step, RIGHT, k] = cur_bg[18 + k, width - 1].astype(bf16)
            bgx_send[step, LEFT, k] = cur_bg[k, 0].astype(bf16)

    def prepare_body_x(step, source):
        for k in range(9):
            bdx_send[step, RIGHT, k] = source[18 + k].astype(bf16)
            bdx_send[step, LEFT, k] = source[k].astype(bf16)

    def stream_bg(step, inner, outer):
        def store(q, x, value):
            p = q if x == 0 else 26 - q
            rd_bg[pl.ds((p * width + x) * depth, depth), :] = value

        stream(
            lambda q, x: cur_bg[q, x],
            lambda w, k: bgx_recv[step, w, k].astype(f32),
            lambda w: pk_recv[step, w - 2].astype(f32),
            bg_first, width, lanes, depth, length, store, inner, outer,
        )

    def stream_body(step):
        source = body if step == 0 else cur_body

        def store(q, x, value):
            rd_body[q] = value

        stream(
            lambda q, x: source[q],
            lambda w, k: bdx_recv[step, w, k].astype(f32),
            lambda w: pk_recv[2 * step, w - 2].astype(f32),
            body_first, 1, lanes, depth, length, store,
        )

    def collide_bg(last):
        for x in range(width):
            def load(q):
                p = q if x == 0 else 26 - q
                return rd_bg[pl.ds((p * width + x) * depth, depth), :]

            def store(q, value):
                if last:
                    out_bg[q, pl.ds(x, depth, stride=width), :] = value
                else:
                    cur_bg[q, x] = value

            collide(load, store)

    group = next(g for g in (16, 8, 4, 2, 1) if jobs % g == 0)

    def contributions(part):
        start = part * EARLY

        def some(i, total):
            for k in range(group):
                j = i * group + k
                d = donor[j]
                first = (start * width + lax.rem(d, width)) * depth + lax.div(d, width)
                picked = rd_bg[pl.ds(first, HALF, stride=width * depth), :]
                product = jnp.dot(picked.astype(bf16), weights[j], preferred_element_type=f32)
                contrib[part, j] = product
                total = total + product
            return total

        total = lax.fori_loop(0, jobs // group, some, jnp.zeros((HALF, length), f32))
        if part == 0:
            total = jnp.where(message_rows < EARLY, total, 0.0)
        return jnp.sum(total, axis=0, keepdims=True)

    def message(part, d, c):
        value = contrib[part, chosen[d * CAP + c]]
        entry = jnp.full((HALF, length), label[d * CAP + c], jnp.int32).astype(f32)
        return jnp.where(message_rows == EARLY, entry, value).astype(bf16)

    def send_contributions(step, part):
        def to(k, carry):
            d = lax.rem(gx + 1 + lax.rem(k - 1 + groups // 2 - 1, groups - 1), groups)
            for c in range(CAP):
                outgoing[step, part, d, pl.ds(c * HALF, HALF), :] = message(part, d, c)
            remote(outgoing.at[step, part, d], arrived.at[step, part, gx], a2a_s.at[step, part],
                   a2a_r.at[step, part], (d, gy)).start()
            return carry

        unrolled(1, groups, to)
        for c in range(CAP):
            arrived[step, part, gx, pl.ds(c * HALF, HALF), :] = message(part, gx, c)

    def wait_bytes(ref, semaphore):
        pltpu.make_async_copy(ref, ref, semaphore).wait()

    def send_sums(step, mass_target, mass_interp):
        both = jnp.concatenate([mass_target, mass_interp], axis=0)
        sum_send[step] = both
        sum_recv[step, me] = both

        def to(k, carry):
            d = lax.rem(me + k, devices)
            remote(sum_send.at[step], sum_recv.at[step, me], tot_s.at[step], tot_r.at[step],
                   (lax.div(d, layers), lax.rem(d, layers))).start()
            return carry

        unrolled(1, devices, to)

    with jax.named_scope("loads"):
        for copy in loads[:7]:
            copy.wait()
    hits = [rows == fringe[r] for r in range(fringe_count)]
    covered = functools.reduce(jnp.logical_or, hits)

    def mass_ahead(source):
        ahead = {0: (mine, ACROSS), 1: (bgx_recv[0, LEFT, 9].astype(f32), ACROSS_LEFT),
                 -1: (bgx_recv[0, RIGHT, 9].astype(f32), ACROSS_RIGHT)}
        held = blank
        for q, (cx, cy, cz) in enumerate(VELOCITY):
            share, way = ahead[cx]
            if cy:
                far = pk_recv[0, way - 2].astype(f32)
                if cy == -1:
                    far = pltpu.roll(far, 1, 1)
                share = jnp.where(lanes == (length - 1 if cy == 1 else 0), far, share)
            if cz:
                share = pltpu.roll(share, (-cz) % depth, 0)
            held = held + share * source[q]
        return jnp.sum(held, axis=0, keepdims=True)

    def gather(step, part):
        wait_bytes(arrived.at[step, part, pl.ds(0, groups - 1)], a2a_r.at[step, part])

        def one(o, totals):
            for c in range(CAP):
                value = arrived[step, part, o, pl.ds(c * HALF, HALF), :].astype(f32)
                entry = value[EARLY : EARLY + 1]
                totals = tuple(
                    t + jnp.where(entry == float(r), value, 0.0) for r, t in enumerate(totals)
                )
            return totals

        zero = jnp.zeros((HALF, length), f32)
        totals = lax.fori_loop(0, groups, one, (zero,) * (2 * fringe_count))
        for r in range(2 * fringe_count):
            interp[part, r] = totals[r]

    def mix(step):
        with jax.named_scope("waitsums"):
            wait_bytes(sum_recv.at[step, pl.ds(0, devices - 1)], tot_r.at[step])
        sums = jnp.sum(jnp.sum(sum_recv[step], axis=0), axis=1, keepdims=True)
        factor = sums[0:1] / sums[1:2]

        def row(r, p):
            part = p >= EARLY
            p -= part * EARLY
            return interp[int(part), r, p : p + 1, :]

        for q in range(27):
            old = rd_body[q]
            fresh = jnp.zeros((depth, length), f32)
            for r in range(fringe_count):
                fresh = jnp.where(hits[r], row(r, q) + row(fringe_count + r, 26 - q), fresh)
            rd_body[q] = jnp.where(covered, 0.5 * (old + factor * fresh), old)

    with jax.named_scope("prep0"):
        for q in range(27):
            for x in range(width):
                cur_bg[q, x] = bg[q, pl.ds(x, depth, stride=width), :]
        mine = covered.astype(f32)
        prepare_bg_x(0)
        for w in ways:
            packed = pack_body(pack_bg(w), body, w)
            pk_send[0, w - 2] = jnp.where(lanes == length - 1, mine, packed).astype(bf16)
        prepare_body_x(0, body)
        for w in (RIGHT, LEFT):
            bgx_send[0, w, 9] = mine.astype(bf16)
        tail = (HALF + EARLY - 27) * width * depth
        rd_bg[pl.ds(27 * width * depth, tail), :] = jnp.zeros((tail, length), f32)
        for part in range(2):
            contrib[part, jobs] = jnp.zeros((HALF, length), f32)

    with jax.named_scope("barrier"):
        pl.semaphore_wait(barrier, devices - 1)
    for copy in packs[0][:1] + bg_x[0] + packs[0][1:]:
        copy.start()

    def choose(d, carry):
        def scan(i, found):
            first, second = found
            for k in range(group):
                j = jobs - 1 - (i * group + k)
                match = target[j] == d
                second = jnp.where(match, first, second)
                first = jnp.where(match, j, first)
            return first, second

        found = lax.fori_loop(0, jobs // group, scan, (jnp.int32(jobs), jnp.int32(jobs)))
        for c in range(CAP):
            chosen[d * CAP + c] = found[c]
            j = jnp.minimum(found[c], jobs - 1)
            held = slot[j] + fringe_count * lax.rem(donor[j], width)
            label[d * CAP + c] = jnp.where(found[c] < jobs, held, -1)
        return carry

    with jax.named_scope("choose"):
        lax.fori_loop(0, groups, choose, 0)

    with jax.named_scope("across0"):
        packs[0][0].wait_recv()
    with jax.named_scope("inner0"):
        stream_bg(0, True, False)
    loads[7].wait()
    with jax.named_scope("early0"):
        first_interp = contributions(0)
    with jax.named_scope("send_early0"):
        send_contributions(0, 0)
    for copy in body_x[0]:
        copy.start()
    with jax.named_scope("halo0"):
        for copy in packs[0][1:] + bg_x[0]:
            copy.wait_recv()
    with jax.named_scope("outer0"):
        stream_bg(0, False, True)
    with jax.named_scope("collide0"):
        collide_bg(False)
    with jax.named_scope("prepare1"):
        prepare_bg_x(1)
        for w in ways:
            pk_send[1, w - 2] = pack_bg(w).astype(bf16)
    for copy in packs[1][:1] + bg_x[1] + packs[1][1:]:
        copy.start()
    with jax.named_scope("late0"):
        mass_interp = first_interp + contributions(1)
    with jax.named_scope("sums0"):
        send_sums(0, mass_ahead(body), mass_interp)
    with jax.named_scope("send_late0"):
        send_contributions(0, 1)

    with jax.named_scope("across1"):
        packs[1][0].wait_recv()
    with jax.named_scope("inner1"):
        stream_bg(1, True, False)
    with jax.named_scope("early1"):
        first_interp = contributions(0)
    with jax.named_scope("gather_early0"):
        gather(0, 0)
    with jax.named_scope("halo1"):
        for copy in packs[1][1:] + bg_x[1]:
            copy.wait_recv()
    with jax.named_scope("send_early1"):
        send_contributions(1, 0)
    with jax.named_scope("outer1"):
        stream_bg(1, False, True)
    with jax.named_scope("late1"):
        mass_interp = first_interp + contributions(1)
    with jax.named_scope("send_late1"):
        send_contributions(1, 1)

    with jax.named_scope("body_halo0"):
        for copy in body_x[0]:
            copy.wait_recv()
    with jax.named_scope("body0"):
        stream_body(0)
    with jax.named_scope("gather_late0"):
        gather(0, 1)
    with jax.named_scope("mix0"):
        mix(0)
    is_solid = solid[...] == 1

    def store_body(q, value):
        cur_body[q] = value

    with jax.named_scope("collide_body0"):
        collide(lambda q: rd_body[q], store_body, is_solid)
    with jax.named_scope("prepare_body1"):
        prepare_body_x(1, cur_body)
        for w in ways:
            pk_send[2, w - 2] = pack_body(blank, cur_body, w).astype(bf16)
    for copy in packs[2][:1] + body_x[1] + packs[2][1:]:
        copy.start()
    with jax.named_scope("sums1"):
        send_sums(1, mass_ahead(cur_body), mass_interp)

    with jax.named_scope("collide1"):
        collide_bg(True)
    with jax.named_scope("gather_early1"):
        gather(1, 0)
    with jax.named_scope("body_halo1"):
        for copy in packs[2] + body_x[1]:
            copy.wait_recv()
    with jax.named_scope("body1"):
        stream_body(1)
    with jax.named_scope("gather_late1"):
        gather(1, 1)
    with jax.named_scope("mix1"):
        mix(1)

    def store_out(q, value):
        out_body[q] = value

    with jax.named_scope("collide_body1"):
        collide(lambda q: rd_body[q], store_out, is_solid)

    with jax.named_scope("drain"):
        for copy in packs[0] + packs[1] + packs[2] + bg_x[0] + bg_x[1] + body_x[0] + body_x[1]:
            copy.wait_send()
        for step in range(STEPS):
            for part in range(2):
                wait_bytes(outgoing.at[step, part, pl.ds(0, groups - 1)], a2a_s.at[step, part])
            wait_bytes(sum_recv.at[step, pl.ds(0, devices - 1)], tot_s.at[step])


def hand_over(bg, body, out_bg, out_body, store_sem):
    stores = []
    for source, out in ((bg, out_bg), (body, out_body)):
        for k in range(3):
            span = pl.ds(9 * k, 9)
            stores.append(pltpu.make_async_copy(source.at[span], out.at[span], store_sem.at[len(stores)]))
    for store in stores:
        store.start()
    for store in stores:
        store.wait()


def local(groups, layers, background, overset_block, solid_mask, donor_tile, target_rank,
          target_slot, fringe_tiles, interp_weights):
    _, depth, width, length = background.shape
    jobs, nodes = interp_weights.shape[2], interp_weights.shape[3]
    assert overset_block.shape[2] == 1 and width == 2 and nodes == length and layers == 2 and STEPS == 2
    fringe_count = fringe_tiles.shape[-1]
    devices = groups * layers
    plane = (depth, length)
    f32, bf16 = jnp.float32, jnp.bfloat16
    vmem, smem = pltpu.VMEM, pltpu.SMEM
    dma = pltpu.SemaphoreType.DMA
    next_bg, next_body = pl.pallas_call(
        functools.partial(kernel, groups, layers, fringe_count),
        out_shape=(
            vmem((27, depth * width, length), f32),
            vmem((27, depth, length), f32),
        ),
        in_specs=[pl.BlockSpec(memory_space=pltpu.HBM)] * 8,
        out_specs=(pl.BlockSpec(memory_space=pltpu.VMEM),) * 2,
        scratch_shapes=[
            smem((jobs,), jnp.int32),
            smem((jobs,), jnp.int32),
            smem((jobs,), jnp.int32),
            smem((fringe_count,), jnp.int32),
            vmem((27, depth * width, length), f32),
            vmem((27, depth, length), f32),
            vmem((depth, length), jnp.int32),
            vmem((jobs, nodes, nodes), bf16),
            dma((8,)),
            vmem((STEPS, 2, 10) + plane, bf16),
            vmem((STEPS, 2, 10) + plane, bf16),
            vmem((STEPS, 2, 9) + plane, bf16),
            vmem((STEPS, 2, 9) + plane, bf16),
            vmem((3, 3) + plane, bf16),
            vmem((3, 3) + plane, bf16),
            vmem((27, width) + plane, f32),
            vmem((27,) + plane, f32),
            vmem(((HALF + EARLY) * width * depth, length), f32),
            vmem((27,) + plane, f32),
            vmem((2, jobs + 1, HALF, length), f32),
            vmem((STEPS, 2, groups, CAP * HALF, length), bf16),
            vmem((STEPS, 2, groups, CAP * HALF, length), bf16),
            vmem((STEPS, 2, length), f32),
            vmem((STEPS, devices, 2, length), f32),
            vmem((2, 2 * fringe_count, HALF, length), f32),
            smem((groups * CAP,), jnp.int32),
            smem((groups * CAP,), jnp.int32),
            dma((17,)),
            dma((17,)),
            dma((STEPS, 2)),
            dma((STEPS, 2)),
            dma((STEPS,)),
            dma((STEPS,)),
        ],
        compiler_params=pltpu.CompilerParams(
            collective_id=0, has_side_effects=True, vmem_limit_bytes=48000000
        ),
    )(*(pltpu.with_memory_space_constraint(a, pltpu.HBM) for a in (
        donor_tile.reshape(jobs),
        target_rank.reshape(jobs),
        target_slot.reshape(jobs),
        fringe_tiles.reshape(fringe_count),
        background.reshape(27, depth * width, length),
        overset_block.reshape(27, depth, length),
        solid_mask.reshape(depth, length),
        interp_weights.reshape(jobs, nodes, nodes),
    )))
    shapes = (
        jax.ShapeDtypeStruct(next_bg.shape, f32),
        jax.ShapeDtypeStruct(next_body.shape, f32),
    )
    next_bg, next_body = pl.pallas_call(
        hand_over,
        out_shape=shapes,
        in_specs=[pl.BlockSpec(memory_space=pltpu.VMEM)] * 2,
        out_specs=(pl.BlockSpec(memory_space=pltpu.HBM),) * 2,
        scratch_shapes=[dma((6,))],
    )(*(pltpu.with_memory_space_constraint(a, pltpu.VMEM) for a in (next_bg, next_body)))
    return next_bg.reshape(background.shape), next_body.reshape(overset_block.shape)


def solution(mesh):
    return jax.shard_map(
        functools.partial(local, mesh.shape["gx"], mesh.shape["gy"]),
        mesh=mesh,
        in_specs=(
            P(None, None, "gx", "gy"),
            P(None, None, "gx", "gy"),
            P(None, "gx", "gy"),
            P("gx", "gy", None),
            P("gx", "gy", None, None),
            P("gx", "gy", None),
            P("gx", "gy", None),
            P("gx", "gy", None, None, None),
        ),
        out_specs=(P(None, None, "gx", "gy"), P(None, None, "gx", "gy")),
        check_vma=False,
    )
```

```python
import functools

import jax
import jax.numpy as jnp
import numpy as np
from jax import lax
from jax.experimental import pallas as pl
from jax.experimental.pallas import tpu as pltpu
from jax.sharding import PartitionSpec as P

CAP = 2
STEPS = 2
RELAXATION = 1.25
HALF = 16
EARLY = 15
MESH = pl.DeviceIdType.MESH

VELOCITY = [(x, y, z) for x in (-1, 0, 1) for y in (-1, 0, 1) for z in (-1, 0, 1)]
WEIGHT = [(8 / 27, 2 / 27, 1 / 54, 1 / 216)[abs(x) + abs(y) + abs(z)] for x, y, z in VELOCITY]

RIGHT, LEFT, ACROSS, ACROSS_RIGHT, ACROSS_LEFT = range(5)


def column_lists(width):
    lists = {ACROSS: [], ACROSS_RIGHT: [], ACROSS_LEFT: []}
    for q, (cx, cy, _) in enumerate(VELOCITY):
        if cy == 0:
            continue
        for x in range(width):
            to = x + cx
            way = ACROSS_RIGHT if to >= width else ACROSS_LEFT if to < 0 else ACROSS
            lists[way].append((q, x))
    return lists


def unrolled(start, stop, body):
    step = next(n for n in (16, 8, 4, 2, 1) if (stop - start) // n >= 1)

    def several(i, carry):
        for k in range(step):
            body(start + i * step + k, 0)
        return carry

    whole = (stop - start) // step
    lax.fori_loop(0, whole, several, 0)
    for k in range(start + whole * step, stop):
        body(k, 0)


def pack_columns(packed, plane, columns, first, lanes, length):
    for k, (q, x) in enumerate(columns, first):
        edge = length - 1 if VELOCITY[q][1] == 1 else 0
        value = plane(q, x)
        if (k - edge) % length:
            value = pltpu.roll(value, (k - edge) % length, 1)
        packed = jnp.where(lanes == k, value, packed)
    return packed


def stream(plane, across_x, packs, first, width, lanes, depth, length, store, inner=True, outer=True):
    lists = column_lists(width)
    where_is = {way: {c: k for k, c in enumerate(cols, first[way])} for way, cols in lists.items()}
    for q, (cx, cy, cz) in enumerate(VELOCITY):
        for x in range(width):
            source = x - cx
            if not (inner if 0 <= source < width else outer):
                continue
            if source < 0:
                value, way, column = across_x(RIGHT, q - 18), ACROSS_RIGHT, (q, width - 1)
            elif source >= width:
                value, way, column = across_x(LEFT, q), ACROSS_LEFT, (q, 0)
            else:
                value, way, column = plane(q, source), ACROSS, (q, source)
            if cy:
                edge = 0 if cy == 1 else length - 1
                k = where_is[way][column]
                far = packs(way)
                if (edge - k) % length:
                    far = pltpu.roll(far, (edge - k) % length, 1)
                value = jnp.where(lanes == edge, far, pltpu.roll(value, cy % length, 1))
            if cz:
                value = pltpu.roll(value, cz % depth, 0)
            store(q, x, value)


def collide(load, store, solid=None):
    density = None
    moment = [None, None, None]
    for q, velocity in enumerate(VELOCITY):
        value = load(q)
        density = value if density is None else density + value
        for axis in range(3):
            if velocity[axis]:
                signed = value if velocity[axis] == 1 else -value
                moment[axis] = signed if moment[axis] is None else moment[axis] + signed
    flow = [m / density for m in moment]
    square = flow[0] * flow[0] + flow[1] * flow[1] + flow[2] * flow[2]
    base = 1.0 - 1.5 * square
    scaled = {w: (RELAXATION * w) * density for w in sorted(set(WEIGHT))}
    for q in range(14):
        along = None
        for axis in range(3):
            if VELOCITY[q][axis]:
                term = flow[axis] if VELOCITY[q][axis] == 1 else -flow[axis]
                along = term if along is None else along + term
        if along is None:
            pairs = [(q, scaled[WEIGHT[q]] * base)]
        else:
            even = scaled[WEIGHT[q]] * (base + 4.5 * along * along)
            odd = scaled[WEIGHT[q]] * (3.0 * along)
            pairs = [(q, even + odd), (26 - q, even - odd)]
        values = [load(p) for p, _ in pairs]
        for (p, equilibrium), value, other in zip(pairs, values, values[::-1]):
            relaxed = (1.0 - RELAXATION) * value + equilibrium
            if solid is not None:
                relaxed = jnp.where(solid, other, relaxed)
            store(p, relaxed)


def kernel(
    groups, layers, fringe_count, *refs,
):
    operands, (out_bg, out_body), loaded, load_sem, *scratch = (
        refs[:8], refs[8:10], refs[10:18], *refs[18:]
    )
    loads = [
        pltpu.make_async_copy(a, b, load_sem.at[i]) for i, (a, b) in enumerate(zip(operands, loaded))
    ]
    for copy in loads:
        copy.start()
    steps(groups, layers, fringe_count, loads, *loaded, out_bg, out_body, *scratch)


def steps(
    groups, layers, fringe_count, loads, donor, target, slot, fringe,
    bg, body, solid, weights, out_bg, out_body,
    bgx_send, bgx_recv, bdx_send, bdx_recv, pk_send, pk_recv,
    cur_bg, cur_body, rd_bg, rd_body, contrib, outgoing, arrived,
    sum_send, sum_recv, interp, gain, chosen, label, span, sent, landed,
):
    gx, gy = lax.axis_index("gx"), lax.axis_index("gy")
    devices = groups * layers
    me = gx * layers + gy
    jobs = weights.shape[0]
    depth, length = cur_body.shape[1], cur_body.shape[2]
    width = cur_bg.shape[1]
    right = lax.rem(gx + 1, groups)
    left = lax.rem(gx + groups - 1, groups)
    other = lax.rem(gy + 1, layers)
    peer = [(right, gy), (left, gy), (gx, other), (right, other), (left, other)]
    f32, bf16 = jnp.float32, jnp.bfloat16

    barrier = pltpu.get_barrier_semaphore()

    def greet(k, carry):
        d = lax.rem(me + k, devices)
        pl.semaphore_signal(
            barrier, inc=1, device_id=(lax.div(d, layers), lax.rem(d, layers)), device_id_type=MESH
        )
        return carry

    with jax.named_scope("greet"):
        unrolled(1, devices, greet)

    lanes = lax.broadcasted_iota(jnp.int32, (depth, length), 1)
    rows = lax.broadcasted_iota(jnp.int32, (depth, length), 0)
    message_rows = lax.broadcasted_iota(jnp.int32, (HALF, length), 0)
    bg_columns = column_lists(width)
    body_columns = column_lists(1)
    ways = (ACROSS, ACROSS_RIGHT, ACROSS_LEFT)
    bg_first = {w: 0 for w in ways}
    body_first = {w: len(bg_columns[w]) for w in ways}
    blank = jnp.zeros((depth, length), f32)

    counts = {"sent": 0}

    def size(ref):
        return int(np.prod(ref.shape)) * jnp.dtype(ref.dtype).itemsize

    def remote(src, dst, phase, to, times=1):
        for key in ("sent", phase):
            counts[key] = counts.get(key, 0) + times * size(src)
        return pltpu.make_async_remote_copy(
            src_ref=src, dst_ref=dst, send_sem=sent, recv_sem=landed.at[phase], device_id=to,
            device_id_type=MESH
        )

    def wait_all(key):
        part = span.at[pl.ds(0, counts[key] // (4 * length))]
        assert counts[key] == size(part)
        pltpu.make_async_copy(part, part, sent if key == "sent" else landed.at[key]).wait()

    def pack_copies(i, phases):
        return [
            remote(pk_send.at[i, w - 2], pk_recv.at[i, w - 2], phase, peer[w])
            for w, phase in zip(ways, phases)
        ]

    def x_copies(send, recv, step, planes, phase):
        return [
            remote(send.at[step, w, pl.ds(0, planes)], recv.at[step, w, pl.ds(0, planes)], phase, peer[w])
            for w in (RIGHT, LEFT)
        ]

    packs = [pack_copies(0, (0, 1, 1)), pack_copies(1, (2, 3, 3)), pack_copies(2, (5, 5, 5))]
    bg_x = [x_copies(bgx_send, bgx_recv, step, 10 - step, 1 + 2 * step) for step in range(STEPS)]
    body_x = [x_copies(bdx_send, bdx_recv, step, 9, 4 + step) for step in range(STEPS)]

    def pack_bg(w):
        return pack_columns(blank, lambda q, x: cur_bg[q, x], bg_columns[w], bg_first[w], lanes, length)

    def pack_body(packed, source, w):
        return pack_columns(packed, lambda q, x: source[q], body_columns[w], body_first[w], lanes, length)

    def prepare_bg_x(step):
        for k in range(9):
            bgx_send[step, RIGHT, k] = cur_bg[18 + k, width - 1].astype(bf16)
            bgx_send[step, LEFT, k] = cur_bg[k, 0].astype(bf16)

    def prepare_body_x(step, source):
        for k in range(9):
            bdx_send[step, RIGHT, k] = source[18 + k].astype(bf16)
            bdx_send[step, LEFT, k] = source[k].astype(bf16)

    def stream_bg(step, inner, outer):
        def store(q, x, value):
            p = q if x == 0 else 26 - q
            rd_bg[pl.ds((p * width + x) * depth, depth), :] = value

        stream(
            lambda q, x: cur_bg[q, x],
            lambda w, k: bgx_recv[step, w, k].astype(f32),
            lambda w: pk_recv[step, w - 2].astype(f32),
            bg_first, width, lanes, depth, length, store, inner, outer,
        )

    def stream_body(step):
        source = body if step == 0 else cur_body

        def store(q, x, value):
            rd_body[q] = value

        stream(
            lambda q, x: source[q],
            lambda w, k: bdx_recv[step, w, k].astype(f32),
            lambda w: pk_recv[2 * step, w - 2].astype(f32),
            body_first, 1, lanes, depth, length, store,
        )

    def collide_bg(last):
        for x in range(width):
            def load(q):
                p = q if x == 0 else 26 - q
                return rd_bg[pl.ds((p * width + x) * depth, depth), :]

            def store(q, value):
                if last:
                    out_bg[q, pl.ds(x, depth, stride=width), :] = value
                else:
                    cur_bg[q, x] = value

            collide(load, store)

    group = next(g for g in (16, 8, 4, 2, 1) if jobs % g == 0)

    def contributions(part):
        start = part * EARLY

        def some(i, total):
            for k in range(group):
                j = i * group + k
                d = donor[j]
                first = (start * width + lax.rem(d, width)) * depth + lax.div(d, width)
                picked = rd_bg[pl.ds(first, HALF, stride=width * depth), :]
                product = jnp.dot(picked.astype(bf16), weights[j], preferred_element_type=f32)
                contrib[part, j] = product
                total = total + product
            return total

        total = lax.fori_loop(0, jobs // group, some, jnp.zeros((HALF, length), f32))
        if part == 0:
            total = jnp.where(message_rows < EARLY, total, 0.0)
        return jnp.sum(total, axis=0, keepdims=True)

    def message(part, d, c):
        value = contrib[part, chosen[d * CAP + c]]
        entry = jnp.full((HALF, length), label[d * CAP + c], jnp.int32).astype(f32)
        return jnp.where(message_rows == EARLY, entry, value).astype(bf16)

    def send_contributions(step, part):
        phase = 6 + 2 * step + part
        counts[phase] = (groups - 1) * CAP * HALF * length * 2
        counts["sent"] += counts[phase]

        def to(k, carry):
            d = lax.rem(gx + 1 + lax.rem(k - 1 + groups // 2 - 1, groups - 1), groups)
            for c in range(CAP):
                outgoing[step, part, d, pl.ds(c * HALF, HALF), :] = message(part, d, c)
            start_one(outgoing.at[step, part, d], arrived.at[step, part, gx], phase, (d, gy))
            return carry

        unrolled(1, groups, to)
        for c in range(CAP):
            arrived[step, part, gx, pl.ds(c * HALF, HALF), :] = message(part, gx, c)

    def start_one(src, dst, phase, to):
        pltpu.make_async_remote_copy(
            src_ref=src, dst_ref=dst, send_sem=sent, recv_sem=landed.at[phase], device_id=to,
            device_id_type=MESH
        ).start()

    def send_sums(step, mass_target, mass_interp):
        both = jnp.concatenate([mass_target, mass_interp], axis=0)
        sum_send[step] = both
        sum_recv[step, me] = both
        phase = 10 + step
        counts[phase] = (devices - 1) * 2 * length * 4
        counts["sent"] += counts[phase]

        def to(k, carry):
            d = lax.rem(me + k, devices)
            start_one(sum_send.at[step], sum_recv.at[step, me], phase, (lax.div(d, layers), lax.rem(d, layers)))
            return carry

        unrolled(1, devices, to)

    with jax.named_scope("loads"):
        for copy in loads[:7]:
            copy.wait()
    hits = [rows == fringe[r] for r in range(fringe_count)]
    covered = functools.reduce(jnp.logical_or, hits)

    def mass_ahead(source):
        ahead = {0: (mine, ACROSS), 1: (bgx_recv[0, LEFT, 9].astype(f32), ACROSS_LEFT),
                 -1: (bgx_recv[0, RIGHT, 9].astype(f32), ACROSS_RIGHT)}
        held = blank
        for q, (cx, cy, cz) in enumerate(VELOCITY):
            share, way = ahead[cx]
            if cy:
                far = pk_recv[0, way - 2].astype(f32)
                if cy == -1:
                    far = pltpu.roll(far, 1, 1)
                share = jnp.where(lanes == (length - 1 if cy == 1 else 0), far, share)
            if cz:
                share = pltpu.roll(share, (-cz) % depth, 0)
            held = held + share * source[q]
        return jnp.sum(held, axis=0, keepdims=True)

    def gather(step, part):
        wait_all(6 + 2 * step + part)
        many = next(n for n in (4, 2, 1) if groups % n == 0)

        def some(i, totals):
            for o in [i * many + k for k in range(many)]:
                for c in range(CAP):
                    value = arrived[step, part, o, pl.ds(c * HALF, HALF), :].astype(f32)
                    entry = value[EARLY : EARLY + 1]
                    totals = tuple(
                        t + jnp.where(entry == float(r), value, 0.0) for r, t in enumerate(totals)
                    )
            return totals

        zero = jnp.zeros((HALF, length), f32)
        totals = lax.fori_loop(0, groups // many, some, (zero,) * (2 * fringe_count))
        for r in range(2 * fringe_count):
            interp[part, r] = totals[r]

    def row(r, p):
        part = p >= EARLY
        p -= part * EARLY
        return interp[int(part), r, p : p + 1, :]

    def halve():
        for q in range(27):
            old = rd_body[q]
            fresh = jnp.zeros((depth, length), f32)
            for r in range(fringe_count):
                fresh = jnp.where(hits[r], row(r, q) + row(fringe_count + r, 26 - q), fresh)
            rd_body[q] = jnp.where(covered, 0.5 * old, old)
            gain[q] = 0.5 * fresh

    def ratio(step):
        wait_all(10 + step)
        sums = jnp.sum(jnp.sum(sum_recv[step], axis=0), axis=1, keepdims=True)
        return sums[0:1] / sums[1:2]

    def mixed(factor):
        return lambda q: jnp.where(covered, rd_body[q] + factor * gain[q], rd_body[q])

    with jax.named_scope("prep0"):
        for q in range(27):
            for x in range(width):
                cur_bg[q, x] = bg[q, pl.ds(x, depth, stride=width), :]
        mine = covered.astype(f32)
        prepare_bg_x(0)
        for w in ways:
            packed = pack_body(pack_bg(w), body, w)
            pk_send[0, w - 2] = jnp.where(lanes == length - 1, mine, packed).astype(bf16)
        prepare_body_x(0, body)
        for w in (RIGHT, LEFT):
            bgx_send[0, w, 9] = mine.astype(bf16)
        tail = (HALF + EARLY - 27) * width * depth
        rd_bg[pl.ds(27 * width * depth, tail), :] = jnp.zeros((tail, length), f32)
        for part in range(2):
            contrib[part, jobs] = jnp.zeros((HALF, length), f32)

    def choose(d, carry):
        def scan(i, found):
            first, second = found
            for k in range(group):
                j = jobs - 1 - (i * group + k)
                match = target[j] == d
                second = jnp.where(match, first, second)
                first = jnp.where(match, j, first)
            return first, second

        found = lax.fori_loop(0, jobs // group, scan, (jnp.int32(jobs), jnp.int32(jobs)))
        for c in range(CAP):
            chosen[d * CAP + c] = found[c]
            j = jnp.minimum(found[c], jobs - 1)
            held = slot[j] + fringe_count * lax.rem(donor[j], width)
            label[d * CAP + c] = jnp.where(found[c] < jobs, held, -1)
        return carry

    is_solid = solid[...] == 1

    def store_body(q, value):
        cur_body[q] = value

    def store_out(q, value):
        out_body[q] = value

    with jax.named_scope("barrier"):
        pl.semaphore_wait(barrier, devices - 1)
    with jax.named_scope("start_halo0"):
        for copy in packs[0][:1] + bg_x[0] + packs[0][1:]:
            copy.start()
    with jax.named_scope("choose"):
        lax.fori_loop(0, groups, choose, 0)
    with jax.named_scope("across0"):
        wait_all(0)
    with jax.named_scope("inner0"):
        stream_bg(0, True, False)
    with jax.named_scope("load7"):
        loads[7].wait()
    with jax.named_scope("early0"):
        first_interp = contributions(0)
    with jax.named_scope("send_early0"):
        send_contributions(0, 0)
    with jax.named_scope("start_body0"):
        for copy in body_x[0]:
            copy.start()
    with jax.named_scope("halo0"):
        wait_all(1)
    with jax.named_scope("outer0"):
        stream_bg(0, False, True)
    with jax.named_scope("collide0"):
        collide_bg(False)
    with jax.named_scope("prepare1"):
        prepare_bg_x(1)
        for copy in bg_x[1]:
            copy.start()
        for w in ways:
            pk_send[1, w - 2] = pack_bg(w).astype(bf16)
        for copy in packs[1]:
            copy.start()
    with jax.named_scope("late0"):
        mass_interp = first_interp + contributions(1)
    with jax.named_scope("sums0"):
        send_sums(0, mass_ahead(body), mass_interp)
    with jax.named_scope("send_late0"):
        send_contributions(0, 1)
    with jax.named_scope("across1"):
        wait_all(2)
    with jax.named_scope("inner1"):
        stream_bg(1, True, False)
    with jax.named_scope("early1"):
        first_interp = contributions(0)
    with jax.named_scope("gather_early0"):
        gather(0, 0)
    with jax.named_scope("halo1"):
        wait_all(3)
    with jax.named_scope("send_early1"):
        send_contributions(1, 0)
    with jax.named_scope("outer1"):
        stream_bg(1, False, True)
    with jax.named_scope("late1"):
        mass_interp = first_interp + contributions(1)
    with jax.named_scope("send_late1"):
        send_contributions(1, 1)
    with jax.named_scope("body_halo0"):
        wait_all(4)
    with jax.named_scope("body0"):
        stream_body(0)
    with jax.named_scope("gather_late0"):
        gather(0, 1)
    with jax.named_scope("halve0"):
        halve()
    with jax.named_scope("ratio0"):
        factor = ratio(0)
    with jax.named_scope("collide_body0"):
        collide(mixed(factor), store_body, is_solid)
    with jax.named_scope("prepare_body1"):
        prepare_body_x(1, cur_body)
        for copy in body_x[1]:
            copy.start()
        for w in ways:
            pk_send[2, w - 2] = pack_body(blank, cur_body, w).astype(bf16)
        for copy in packs[2]:
            copy.start()
    with jax.named_scope("sums1"):
        send_sums(1, mass_ahead(cur_body), mass_interp)
    with jax.named_scope("collide1"):
        collide_bg(True)
    with jax.named_scope("gather_early1"):
        gather(1, 0)
    with jax.named_scope("gather_late1"):
        gather(1, 1)
    with jax.named_scope("body_halo1"):
        wait_all(5)
    with jax.named_scope("body1"):
        stream_body(1)
    with jax.named_scope("halve1"):
        halve()
    with jax.named_scope("ratio1"):
        factor = ratio(1)
    with jax.named_scope("collide_body1"):
        collide(mixed(factor), store_out, is_solid)
    with jax.named_scope("drain"):
        wait_all("sent")


def hand_over(bg, body, out_bg, out_body, store_sem):
    stores = []
    for source, out in ((bg, out_bg), (body, out_body)):
        stores.append(pltpu.make_async_copy(source, out, store_sem.at[len(stores)]))
    for store in stores:
        store.start()
    for store in stores:
        store.wait()


def local(groups, layers, background, overset_block, solid_mask, donor_tile, target_rank,
          target_slot, fringe_tiles, interp_weights):
    _, depth, width, length = background.shape
    jobs, nodes = interp_weights.shape[2], interp_weights.shape[3]
    assert overset_block.shape[2] == 1 and width == 2 and nodes == length and layers == 2 and STEPS == 2
    fringe_count = fringe_tiles.shape[-1]
    devices = groups * layers
    plane = (depth, length)
    f32, bf16 = jnp.float32, jnp.bfloat16
    vmem, smem = pltpu.VMEM, pltpu.SMEM
    dma = pltpu.SemaphoreType.DMA
    span_rows = STEPS * (2 * groups * CAP * HALF + 2 * devices + 64 * depth)
    next_bg, next_body = pl.pallas_call(
        functools.partial(kernel, groups, layers, fringe_count),
        out_shape=(
            vmem((27, depth * width, length), f32),
            vmem((27, depth, length), f32),
        ),
        in_specs=[pl.BlockSpec(memory_space=pltpu.HBM)] * 8,
        out_specs=(pl.BlockSpec(memory_space=pltpu.VMEM),) * 2,
        scratch_shapes=[
            smem((jobs,), jnp.int32),
            smem((jobs,), jnp.int32),
            smem((jobs,), jnp.int32),
            smem((fringe_count,), jnp.int32),
            vmem((27, depth * width, length), f32),
            vmem((27, depth, length), f32),
            vmem((depth, length), jnp.int32),
            vmem((jobs, nodes, nodes), bf16),
            dma((8,)),
            vmem((STEPS, 2, 10) + plane, bf16),
            vmem((STEPS, 2, 10) + plane, bf16),
            vmem((STEPS, 2, 9) + plane, bf16),
            vmem((STEPS, 2, 9) + plane, bf16),
            vmem((3, 3) + plane, bf16),
            vmem((3, 3) + plane, bf16),
            vmem((27, width) + plane, f32),
            vmem((27,) + plane, f32),
            vmem(((HALF + EARLY) * width * depth, length), f32),
            vmem((27,) + plane, f32),
            vmem((2, jobs + 1, HALF, length), f32),
            vmem((STEPS, 2, groups, CAP * HALF, length), bf16),
            vmem((STEPS, 2, groups, CAP * HALF, length), bf16),
            vmem((STEPS, 2, length), f32),
            vmem((STEPS, devices, 2, length), f32),
            vmem((2, 2 * fringe_count, HALF, length), f32),
            vmem((27,) + plane, f32),
            smem((groups * CAP,), jnp.int32),
            smem((groups * CAP,), jnp.int32),
            vmem((span_rows, length), f32),
            dma(()),
            dma((12,)),
        ],
        compiler_params=pltpu.CompilerParams(
            collective_id=0, has_side_effects=True, vmem_limit_bytes=48000000
        ),
    )(*(pltpu.with_memory_space_constraint(a, pltpu.HBM) for a in (
        donor_tile.reshape(jobs),
        target_rank.reshape(jobs),
        target_slot.reshape(jobs),
        fringe_tiles.reshape(fringe_count),
        background.reshape(27, depth * width, length),
        overset_block.reshape(27, depth, length),
        solid_mask.reshape(depth, length),
        interp_weights.reshape(jobs, nodes, nodes),
    )))
    shapes = (
        jax.ShapeDtypeStruct(next_bg.shape, f32),
        jax.ShapeDtypeStruct(next_body.shape, f32),
    )
    next_bg, next_body = pl.pallas_call(
        hand_over,
        out_shape=shapes,
        in_specs=[pl.BlockSpec(memory_space=pltpu.VMEM)] * 2,
        out_specs=(pl.BlockSpec(memory_space=pltpu.HBM),) * 2,
        scratch_shapes=[dma((2,))],
    )(*(pltpu.with_memory_space_constraint(a, pltpu.VMEM) for a in (next_bg, next_body)))
    return next_bg.reshape(background.shape), next_body.reshape(overset_block.shape)


def solution(mesh):
    return jax.shard_map(
        functools.partial(local, mesh.shape["gx"], mesh.shape["gy"]),
        mesh=mesh,
        in_specs=(
            P(None, None, "gx", "gy"),
            P(None, None, "gx", "gy"),
            P(None, "gx", "gy"),
            P("gx", "gy", None),
            P("gx", "gy", None, None),
            P("gx", "gy", None),
            P("gx", "gy", None),
            P("gx", "gy", None, None, None),
        ),
        out_specs=(P(None, None, "gx", "gy"), P(None, None, "gx", "gy")),
        check_vma=False,
    )
```

```python
import functools

import jax
import jax.numpy as jnp
import numpy as np
from jax import lax
from jax.experimental import pallas as pl
from jax.experimental.pallas import tpu as pltpu
from jax.sharding import PartitionSpec as P

CAP = 2
STEPS = 2
RELAXATION = 1.25
HALF = 16
EARLY = 15
MESH = pl.DeviceIdType.MESH

VELOCITY = [(x, y, z) for x in (-1, 0, 1) for y in (-1, 0, 1) for z in (-1, 0, 1)]
WEIGHT = [(8 / 27, 2 / 27, 1 / 54, 1 / 216)[abs(x) + abs(y) + abs(z)] for x, y, z in VELOCITY]

RIGHT, LEFT, ACROSS, ACROSS_RIGHT, ACROSS_LEFT = range(5)


def column_lists(width):
    lists = {ACROSS: [], ACROSS_RIGHT: [], ACROSS_LEFT: []}
    for q, (cx, cy, _) in enumerate(VELOCITY):
        if cy == 0:
            continue
        for x in range(width):
            to = x + cx
            way = ACROSS_RIGHT if to >= width else ACROSS_LEFT if to < 0 else ACROSS
            lists[way].append((q, x))
    return lists


def unrolled(start, stop, body):
    step = next(n for n in (16, 8, 4, 2, 1) if (stop - start) // n >= 1)

    def several(i, carry):
        for k in range(step):
            body(start + i * step + k, 0)
        return carry

    whole = (stop - start) // step
    lax.fori_loop(0, whole, several, 0)
    for k in range(start + whole * step, stop):
        body(k, 0)


def pack_columns(packed, plane, columns, first, lanes, length):
    for k, (q, x) in enumerate(columns, first):
        edge = length - 1 if VELOCITY[q][1] == 1 else 0
        value = plane(q, x)
        if (k - edge) % length:
            value = pltpu.roll(value, (k - edge) % length, 1)
        packed = jnp.where(lanes == k, value, packed)
    return packed


def stream(plane, across_x, packs, first, width, lanes, depth, length, store, inner=True, outer=True):
    lists = column_lists(width)
    where_is = {way: {c: k for k, c in enumerate(cols, first[way])} for way, cols in lists.items()}
    for q, (cx, cy, cz) in enumerate(VELOCITY):
        for x in range(width):
            source = x - cx
            if not (inner if 0 <= source < width else outer):
                continue
            if source < 0:
                value, way, column = across_x(RIGHT, q - 18), ACROSS_RIGHT, (q, width - 1)
            elif source >= width:
                value, way, column = across_x(LEFT, q), ACROSS_LEFT, (q, 0)
            else:
                value, way, column = plane(q, source), ACROSS, (q, source)
            if cy:
                edge = 0 if cy == 1 else length - 1
                k = where_is[way][column]
                far = packs(way)
                if (edge - k) % length:
                    far = pltpu.roll(far, (edge - k) % length, 1)
                value = jnp.where(lanes == edge, far, pltpu.roll(value, cy % length, 1))
            if cz:
                value = pltpu.roll(value, cz % depth, 0)
            store(q, x, value)


def collide(load, store, solid=None):
    density = None
    moment = [None, None, None]
    for q, velocity in enumerate(VELOCITY):
        value = load(q)
        density = value if density is None else density + value
        for axis in range(3):
            if velocity[axis]:
                signed = value if velocity[axis] == 1 else -value
                moment[axis] = signed if moment[axis] is None else moment[axis] + signed
    flow = [m / density for m in moment]
    square = flow[0] * flow[0] + flow[1] * flow[1] + flow[2] * flow[2]
    base = 1.0 - 1.5 * square
    scaled = {w: (RELAXATION * w) * density for w in sorted(set(WEIGHT))}
    for q in range(14):
        along = None
        for axis in range(3):
            if VELOCITY[q][axis]:
                term = flow[axis] if VELOCITY[q][axis] == 1 else -flow[axis]
                along = term if along is None else along + term
        if along is None:
            pairs = [(q, scaled[WEIGHT[q]] * base)]
        else:
            even = scaled[WEIGHT[q]] * (base + 4.5 * along * along)
            odd = scaled[WEIGHT[q]] * (3.0 * along)
            pairs = [(q, even + odd), (26 - q, even - odd)]
        values = [load(p) for p, _ in pairs]
        for (p, equilibrium), value, other in zip(pairs, values, values[::-1]):
            relaxed = (1.0 - RELAXATION) * value + equilibrium
            if solid is not None:
                relaxed = jnp.where(solid, other, relaxed)
            store(p, relaxed)


def kernel(
    groups, layers, fringe_count, *refs,
):
    operands, outs, loaded, load_sem, *scratch = (
        refs[:8], refs[8:12], refs[12:20], *refs[20:]
    )
    loads = [
        pltpu.make_async_copy(a, b, load_sem.at[min(i, 4) if i < 7 else 5])
        for i, (a, b) in enumerate(zip(operands, loaded))
    ]
    for copy in loads:
        copy.start()
    steps(groups, layers, fringe_count, loads, load_sem, *loaded, *outs, *scratch)


def steps(
    groups, layers, fringe_count, loads, load_sem, donor, target, slot, fringe,
    bg, body, solid, weights, out_bg, rd_body, gain, state,
    bgx_send, bgx_recv, bdx_send, bdx_recv, pk_send, pk_recv,
    cur_bg, cur_body, rd_bg, contrib, outgoing, arrived,
    sum_send, sum_recv, interp, chosen, label, span, sent, landed,
):
    gx, gy = lax.axis_index("gx"), lax.axis_index("gy")
    devices = groups * layers
    me = gx * layers + gy
    jobs = weights.shape[0]
    depth, length = cur_body.shape[1], cur_body.shape[2]
    width = cur_bg.shape[1]
    right = lax.rem(gx + 1, groups)
    left = lax.rem(gx + groups - 1, groups)
    other = lax.rem(gy + 1, layers)
    peer = [(right, gy), (left, gy), (gx, other), (right, other), (left, other)]
    f32, bf16 = jnp.float32, jnp.bfloat16

    barrier = pltpu.get_barrier_semaphore()

    def greet(k, carry):
        d = lax.rem(me + k, devices)
        pl.semaphore_signal(
            barrier, inc=1, device_id=(lax.div(d, layers), lax.rem(d, layers)), device_id_type=MESH
        )
        return carry

    with jax.named_scope("greet"):
        unrolled(1, devices, greet)

    lanes = lax.broadcasted_iota(jnp.int32, (depth, length), 1)
    rows = lax.broadcasted_iota(jnp.int32, (depth, length), 0)
    message_rows = lax.broadcasted_iota(jnp.int32, (HALF, length), 0)
    bg_columns = column_lists(width)
    body_columns = column_lists(1)
    ways = (ACROSS, ACROSS_RIGHT, ACROSS_LEFT)
    bg_first = {w: 0 for w in ways}
    body_first = {w: len(bg_columns[w]) for w in ways}
    blank = jnp.zeros((depth, length), f32)

    counts = {"sent": 0}

    def size(ref):
        return int(np.prod(ref.shape)) * jnp.dtype(ref.dtype).itemsize

    def remote(src, dst, phase, to, times=1):
        for key in ("sent", phase):
            counts[key] = counts.get(key, 0) + times * size(src)
        return pltpu.make_async_remote_copy(
            src_ref=src, dst_ref=dst, send_sem=sent, recv_sem=landed.at[phase], device_id=to,
            device_id_type=MESH
        )

    def wait_all(key):
        part = span.at[pl.ds(0, counts[key] // (4 * length))]
        assert counts[key] == size(part)
        pltpu.make_async_copy(part, part, sent if key == "sent" else landed.at[key]).wait()

    def pack_copies(i, phases):
        return [
            remote(pk_send.at[i, w - 2], pk_recv.at[i, w - 2], phase, peer[w])
            for w, phase in zip(ways, phases)
        ]

    def x_copies(send, recv, step, planes, phase):
        return [
            remote(send.at[step, w, pl.ds(0, planes)], recv.at[step, w, pl.ds(0, planes)], phase, peer[w])
            for w in (RIGHT, LEFT)
        ]

    packs = [pack_copies(0, (0, 1, 1)), pack_copies(1, (2, 3, 3)), pack_copies(2, (5, 5, 5))]
    bg_x = [x_copies(bgx_send, bgx_recv, step, 10 - step, 1 + 2 * step) for step in range(STEPS)]
    body_x = [x_copies(bdx_send, bdx_recv, step, 9, 4 + step) for step in range(STEPS)]

    def pack_bg(w):
        return pack_columns(blank, lambda q, x: cur_bg[q, x], bg_columns[w], bg_first[w], lanes, length)

    def pack_body(packed, source, w):
        return pack_columns(packed, lambda q, x: source[q], body_columns[w], body_first[w], lanes, length)

    def prepare_bg_x(step):
        for k in range(9):
            bgx_send[step, RIGHT, k] = cur_bg[18 + k, width - 1].astype(bf16)
            bgx_send[step, LEFT, k] = cur_bg[k, 0].astype(bf16)

    def prepare_body_x(step, source):
        for k in range(9):
            bdx_send[step, RIGHT, k] = source[18 + k].astype(bf16)
            bdx_send[step, LEFT, k] = source[k].astype(bf16)

    def stream_bg(step, inner, outer):
        def store(q, x, value):
            p = q if x == 0 else 26 - q
            rd_bg[pl.ds((p * width + x) * depth, depth), :] = value

        stream(
            lambda q, x: cur_bg[q, x],
            lambda w, k: bgx_recv[step, w, k].astype(f32),
            lambda w: pk_recv[step, w - 2].astype(f32),
            bg_first, width, lanes, depth, length, store, inner, outer,
        )

    def stream_body(step):
        source = body if step == 0 else cur_body

        def store(q, x, value):
            rd_body[q] = value

        stream(
            lambda q, x: source[q],
            lambda w, k: bdx_recv[step, w, k].astype(f32),
            lambda w: pk_recv[2 * step, w - 2].astype(f32),
            body_first, 1, lanes, depth, length, store,
        )

    def collide_bg(last):
        for x in range(width):
            def load(q):
                p = q if x == 0 else 26 - q
                return rd_bg[pl.ds((p * width + x) * depth, depth), :]

            def store(q, value):
                if last:
                    out_bg[q, pl.ds(x, depth, stride=width), :] = value
                else:
                    cur_bg[q, x] = value

            collide(load, store)

    group = next(g for g in (16, 8, 4, 2, 1) if jobs % g == 0)

    def contributions(part):
        start = part * EARLY

        def some(i, total):
            for k in range(group):
                j = i * group + k
                d = donor[j]
                first = (start * width + lax.rem(d, width)) * depth + lax.div(d, width)
                picked = rd_bg[pl.ds(first, HALF, stride=width * depth), :]
                product = jnp.dot(picked.astype(bf16), weights[j], preferred_element_type=f32)
                contrib[part, j] = product
                total = total + product
            return total

        total = lax.fori_loop(0, jobs // group, some, jnp.zeros((HALF, length), f32))
        if part == 0:
            total = jnp.where(message_rows < EARLY, total, 0.0)
        return jnp.sum(total, axis=0, keepdims=True)

    def message(part, d, c):
        value = contrib[part, chosen[d * CAP + c]]
        entry = jnp.full((HALF, length), label[d * CAP + c], jnp.int32).astype(f32)
        return jnp.where(message_rows == EARLY, entry, value).astype(bf16)

    def send_contributions(step, part):
        phase = 6 + 2 * step + part
        counts[phase] = (groups - 1) * CAP * HALF * length * 2
        counts["sent"] += counts[phase]

        def to(k, carry):
            d = lax.bitwise_xor(gx, groups - k) if groups & (groups - 1) == 0 else lax.rem(gx + k, groups)
            for c in range(CAP):
                outgoing[step, part, d, pl.ds(c * HALF, HALF), :] = message(part, d, c)
            start_one(outgoing.at[step, part, d], arrived.at[step, part, gx], phase, (d, gy))
            return carry

        unrolled(1, groups, to)
        for c in range(CAP):
            arrived[step, part, gx, pl.ds(c * HALF, HALF), :] = message(part, gx, c)

    def start_one(src, dst, phase, to):
        pltpu.make_async_remote_copy(
            src_ref=src, dst_ref=dst, send_sem=sent, recv_sem=landed.at[phase], device_id=to,
            device_id_type=MESH
        ).start()

    def send_sums(step, mass_target, mass_interp):
        both = jnp.concatenate([mass_target, mass_interp], axis=0)
        sum_send[step] = both
        sum_recv[step, me] = both
        phase = 10 + step
        counts[phase] = (devices - 1) * 2 * length * 4
        counts["sent"] += counts[phase]

        def to(k, carry):
            d = lax.rem(me + k, devices)
            start_one(sum_send.at[step], sum_recv.at[step, me], phase, (lax.div(d, layers), lax.rem(d, layers)))
            return carry

        unrolled(1, devices, to)

    with jax.named_scope("loads"):
        for copy in loads[:4]:
            copy.wait()
        part = span.at[pl.ds(0, (size(bg) + size(body) + size(solid)) // (4 * length))]
        pltpu.make_async_copy(part, part, load_sem.at[4]).wait()
    hits = [rows == fringe[r] for r in range(fringe_count)]
    covered = functools.reduce(jnp.logical_or, hits)

    def mass_ahead(source):
        ahead = {0: (mine, ACROSS), 1: (bgx_recv[0, LEFT, 9].astype(f32), ACROSS_LEFT),
                 -1: (bgx_recv[0, RIGHT, 9].astype(f32), ACROSS_RIGHT)}
        held = blank
        for q, (cx, cy, cz) in enumerate(VELOCITY):
            share, way = ahead[cx]
            if cy:
                far = pk_recv[0, way - 2].astype(f32)
                if cy == -1:
                    far = pltpu.roll(far, 1, 1)
                share = jnp.where(lanes == (length - 1 if cy == 1 else 0), far, share)
            if cz:
                share = pltpu.roll(share, (-cz) % depth, 0)
            held = held + share * source[q]
        return jnp.sum(held, axis=0, keepdims=True)

    def gather(step, part):
        wait_all(6 + 2 * step + part)
        many = next(n for n in (4, 2, 1) if groups % n == 0)

        def some(i, totals):
            for o in [i * many + k for k in range(many)]:
                for c in range(CAP):
                    value = arrived[step, part, o, pl.ds(c * HALF, HALF), :].astype(f32)
                    entry = value[EARLY : EARLY + 1]
                    totals = tuple(
                        t + jnp.where(entry == float(r), value, 0.0) for r, t in enumerate(totals)
                    )
            return totals

        zero = jnp.zeros((HALF, length), f32)
        totals = lax.fori_loop(0, groups // many, some, (zero,) * (2 * fringe_count))
        for r in range(2 * fringe_count):
            interp[part, r] = totals[r]

    def row(r, p):
        part = p >= EARLY
        p -= part * EARLY
        return interp[int(part), r, p : p + 1, :]

    def halve():
        for q in range(27):
            old = rd_body[q]
            fresh = jnp.zeros((depth, length), f32)
            for r in range(fringe_count):
                fresh = jnp.where(hits[r], row(r, q) + row(fringe_count + r, 26 - q), fresh)
            rd_body[q] = jnp.where(covered, 0.5 * old, old)
            gain[q] = 0.5 * fresh

    def ratio(step):
        wait_all(10 + step)
        sums = jnp.sum(jnp.sum(sum_recv[step], axis=0), axis=1, keepdims=True)
        return sums[0:1] / sums[1:2]

    def mixed(factor):
        return lambda q: jnp.where(covered, rd_body[q] + factor * gain[q], rd_body[q])

    with jax.named_scope("prep0"):
        for q in range(27):
            for x in range(width):
                cur_bg[q, x] = bg[q, pl.ds(x, depth, stride=width), :]
        mine = covered.astype(f32)
        prepare_bg_x(0)
        for w in ways:
            packed = pack_body(pack_bg(w), body, w)
            pk_send[0, w - 2] = jnp.where(lanes == length - 1, mine, packed).astype(bf16)
        prepare_body_x(0, body)
        for w in (RIGHT, LEFT):
            bgx_send[0, w, 9] = mine.astype(bf16)
        tail = (HALF + EARLY - 27) * width * depth
        rd_bg[pl.ds(27 * width * depth, tail), :] = jnp.zeros((tail, length), f32)
        for part in range(2):
            contrib[part, jobs] = jnp.zeros((HALF, length), f32)

    def choose(d, carry):
        def scan(i, found):
            first, second = found
            for k in range(group):
                j = jobs - 1 - (i * group + k)
                match = target[j] == d
                second = jnp.where(match, first, second)
                first = jnp.where(match, j, first)
            return first, second

        found = lax.fori_loop(0, jobs // group, scan, (jnp.int32(jobs), jnp.int32(jobs)))
        for c in range(CAP):
            chosen[d * CAP + c] = found[c]
            j = jnp.minimum(found[c], jobs - 1)
            held = slot[j] + fringe_count * lax.rem(donor[j], width)
            label[d * CAP + c] = jnp.where(found[c] < jobs, held, -1)
        return carry

    is_solid = solid[...] == 1

    def store_body(q, value):
        cur_body[q] = value

    with jax.named_scope("barrier"):
        pl.semaphore_wait(barrier, devices - 1)
    with jax.named_scope("start_halo0"):
        for copy in packs[0][:1] + bg_x[0] + packs[0][1:]:
            copy.start()
    with jax.named_scope("choose"):
        lax.fori_loop(0, groups, choose, 0)
    with jax.named_scope("across0"):
        wait_all(0)
    with jax.named_scope("inner0"):
        stream_bg(0, True, False)
    with jax.named_scope("load7"):
        loads[7].wait()
    with jax.named_scope("early0"):
        first_interp = contributions(0)
    with jax.named_scope("send_early0"):
        send_contributions(0, 0)
    with jax.named_scope("start_body0"):
        for copy in body_x[0]:
            copy.start()
    with jax.named_scope("halo0"):
        wait_all(1)
    with jax.named_scope("outer0"):
        stream_bg(0, False, True)
    with jax.named_scope("collide0"):
        collide_bg(False)
    with jax.named_scope("prepare1"):
        prepare_bg_x(1)
        for copy in bg_x[1]:
            copy.start()
        for w in ways:
            pk_send[1, w - 2] = pack_bg(w).astype(bf16)
        for copy in packs[1]:
            copy.start()
    with jax.named_scope("late0"):
        mass_interp = first_interp + contributions(1)
    with jax.named_scope("sums0"):
        send_sums(0, mass_ahead(body), mass_interp)
    with jax.named_scope("send_late0"):
        send_contributions(0, 1)
    with jax.named_scope("across1"):
        wait_all(2)
    with jax.named_scope("inner1"):
        stream_bg(1, True, False)
    with jax.named_scope("early1"):
        first_interp = contributions(0)
    with jax.named_scope("gather_early0"):
        gather(0, 0)
    with jax.named_scope("halo1"):
        wait_all(3)
    with jax.named_scope("send_early1"):
        send_contributions(1, 0)
    with jax.named_scope("outer1"):
        stream_bg(1, False, True)
    with jax.named_scope("late1"):
        mass_interp = first_interp + contributions(1)
    with jax.named_scope("send_late1"):
        send_contributions(1, 1)
    with jax.named_scope("body_halo0"):
        wait_all(4)
    with jax.named_scope("body0"):
        stream_body(0)
    with jax.named_scope("gather_late0"):
        gather(0, 1)
    with jax.named_scope("halve0"):
        halve()
    with jax.named_scope("ratio0"):
        factor = ratio(0)
    with jax.named_scope("collide_body0"):
        collide(mixed(factor), store_body, is_solid)
    with jax.named_scope("prepare_body1"):
        prepare_body_x(1, cur_body)
        for copy in body_x[1]:
            copy.start()
        for w in ways:
            pk_send[2, w - 2] = pack_body(blank, cur_body, w).astype(bf16)
        for copy in packs[2]:
            copy.start()
    with jax.named_scope("sums1"):
        send_sums(1, mass_ahead(cur_body), mass_interp)
    with jax.named_scope("collide1"):
        collide_bg(True)
    with jax.named_scope("gather_early1"):
        gather(1, 0)
    with jax.named_scope("gather_late1"):
        gather(1, 1)
    with jax.named_scope("body_halo1"):
        wait_all(5)
    with jax.named_scope("body1"):
        stream_body(1)
    with jax.named_scope("halve1"):
        halve()
    with jax.named_scope("ratio1"):
        state[1] = mine
        state[2] = is_solid.astype(f32)
        state[0] = jnp.broadcast_to(ratio(1), (depth, length))
    with jax.named_scope("drain"):
        wait_all("sent")


def finish(bg, body, gain, state, out_bg, out_body, done, sems):
    stores = [
        pltpu.make_async_copy(a, b, sems.at[i]) for i, (a, b) in enumerate(((bg, out_bg), (done, out_body)))
    ]
    stores[0].start()
    factor, covered, solid = state[0], state[1] > 0.5, state[2] > 0.5

    def store(q, value):
        done[q] = value

    collide(lambda q: jnp.where(covered, body[q] + factor * gain[q], body[q]), store, solid)
    stores[1].start()
    for copy in stores:
        copy.wait()


def local(groups, layers, background, overset_block, solid_mask, donor_tile, target_rank,
          target_slot, fringe_tiles, interp_weights):
    _, depth, width, length = background.shape
    jobs, nodes = interp_weights.shape[2], interp_weights.shape[3]
    assert overset_block.shape[2] == 1 and width == 2 and nodes == length and layers == 2 and STEPS == 2
    fringe_count = fringe_tiles.shape[-1]
    devices = groups * layers
    plane = (depth, length)
    f32, bf16 = jnp.float32, jnp.bfloat16
    vmem, smem = pltpu.VMEM, pltpu.SMEM
    dma = pltpu.SemaphoreType.DMA
    span_rows = STEPS * (2 * groups * CAP * HALF + 2 * devices + 64 * depth)
    held = pl.pallas_call(
        functools.partial(kernel, groups, layers, fringe_count),
        out_shape=(
            vmem((27, depth * width, length), f32),
            vmem((27,) + plane, f32),
            vmem((27,) + plane, f32),
            vmem((3,) + plane, f32),
        ),
        in_specs=[pl.BlockSpec(memory_space=pltpu.HBM)] * 8,
        out_specs=(pl.BlockSpec(memory_space=pltpu.VMEM),) * 4,
        scratch_shapes=[
            smem((jobs,), jnp.int32),
            smem((jobs,), jnp.int32),
            smem((jobs,), jnp.int32),
            smem((fringe_count,), jnp.int32),
            vmem((27, depth * width, length), f32),
            vmem((27, depth, length), f32),
            vmem((depth, length), jnp.int32),
            vmem((jobs, nodes, nodes), bf16),
            dma((6,)),
            vmem((STEPS, 2, 10) + plane, bf16),
            vmem((STEPS, 2, 10) + plane, bf16),
            vmem((STEPS, 2, 9) + plane, bf16),
            vmem((STEPS, 2, 9) + plane, bf16),
            vmem((3, 3) + plane, bf16),
            vmem((3, 3) + plane, bf16),
            vmem((27, width) + plane, f32),
            vmem((27,) + plane, f32),
            vmem(((HALF + EARLY) * width * depth, length), f32),
            vmem((2, jobs + 1, HALF, length), f32),
            vmem((STEPS, 2, groups, CAP * HALF, length), bf16),
            vmem((STEPS, 2, groups, CAP * HALF, length), bf16),
            vmem((STEPS, 2, length), f32),
            vmem((STEPS, devices, 2, length), f32),
            vmem((2, 2 * fringe_count, HALF, length), f32),
            smem((groups * CAP,), jnp.int32),
            smem((groups * CAP,), jnp.int32),
            vmem((span_rows, length), f32),
            dma(()),
            dma((12,)),
        ],
        compiler_params=pltpu.CompilerParams(
            collective_id=0, has_side_effects=True, vmem_limit_bytes=48000000
        ),
    )(*(pltpu.with_memory_space_constraint(a, pltpu.HBM) for a in (
        donor_tile.reshape(jobs),
        target_rank.reshape(jobs),
        target_slot.reshape(jobs),
        fringe_tiles.reshape(fringe_count),
        background.reshape(27, depth * width, length),
        overset_block.reshape(27, depth, length),
        solid_mask.reshape(depth, length),
        interp_weights.reshape(jobs, nodes, nodes),
    )))
    next_bg, next_body = pl.pallas_call(
        finish,
        out_shape=(
            jax.ShapeDtypeStruct((27, depth * width, length), f32),
            jax.ShapeDtypeStruct((27, depth, length), f32),
        ),
        in_specs=[pl.BlockSpec(memory_space=pltpu.VMEM)] * 4,
        out_specs=(pl.BlockSpec(memory_space=pltpu.HBM),) * 2,
        scratch_shapes=[vmem((27,) + plane, f32), dma((2,))],
    )(*(pltpu.with_memory_space_constraint(a, pltpu.VMEM) for a in held))
    return next_bg.reshape(background.shape), next_body.reshape(overset_block.shape)


def solution(mesh):
    return jax.shard_map(
        functools.partial(local, mesh.shape["gx"], mesh.shape["gy"]),
        mesh=mesh,
        in_specs=(
            P(None, None, "gx", "gy"),
            P(None, None, "gx", "gy"),
            P(None, "gx", "gy"),
            P("gx", "gy", None),
            P("gx", "gy", None, None),
            P("gx", "gy", None),
            P("gx", "gy", None),
            P("gx", "gy", None, None, None),
        ),
        out_specs=(P(None, None, "gx", "gy"), P(None, None, "gx", "gy")),
        check_vma=False,
    )
```

```python
import functools

import jax
import jax.numpy as jnp
import numpy as np
from jax import lax
from jax.experimental import pallas as pl
from jax.experimental.pallas import tpu as pltpu
from jax.sharding import PartitionSpec as P

CAP = 2
STEPS = 2
RELAXATION = 1.25
HALF = 16
EARLY = 15
MESH = pl.DeviceIdType.MESH

VELOCITY = [(x, y, z) for x in (-1, 0, 1) for y in (-1, 0, 1) for z in (-1, 0, 1)]
WEIGHT = [(8 / 27, 2 / 27, 1 / 54, 1 / 216)[abs(x) + abs(y) + abs(z)] for x, y, z in VELOCITY]

RIGHT, LEFT, ACROSS, ACROSS_RIGHT, ACROSS_LEFT = range(5)


def column_lists(width):
    lists = {ACROSS: [], ACROSS_RIGHT: [], ACROSS_LEFT: []}
    for q, (cx, cy, _) in enumerate(VELOCITY):
        if cy == 0:
            continue
        for x in range(width):
            to = x + cx
            way = ACROSS_RIGHT if to >= width else ACROSS_LEFT if to < 0 else ACROSS
            lists[way].append((q, x))
    return lists


def unrolled(start, stop, body):
    step = next(n for n in (16, 8, 4, 2, 1) if (stop - start) // n >= 1)

    def several(i, carry):
        for k in range(step):
            body(start + i * step + k, 0)
        return carry

    whole = (stop - start) // step
    lax.fori_loop(0, whole, several, 0)
    for k in range(start + whole * step, stop):
        body(k, 0)


def pack_columns(packed, plane, columns, first, lanes, length):
    for k, (q, x) in enumerate(columns, first):
        edge = length - 1 if VELOCITY[q][1] == 1 else 0
        value = plane(q, x)
        if (k - edge) % length:
            value = pltpu.roll(value, (k - edge) % length, 1)
        packed = jnp.where(lanes == k, value, packed)
    return packed


def stream(plane, across_x, packs, first, width, lanes, depth, length, store, inner=True, outer=True):
    lists = column_lists(width)
    where_is = {way: {c: k for k, c in enumerate(cols, first[way])} for way, cols in lists.items()}
    for q, (cx, cy, cz) in enumerate(VELOCITY):
        for x in range(width):
            source = x - cx
            if not (inner if 0 <= source < width else outer):
                continue
            if source < 0:
                value, way, column = across_x(RIGHT, q - 18), ACROSS_RIGHT, (q, width - 1)
            elif source >= width:
                value, way, column = across_x(LEFT, q), ACROSS_LEFT, (q, 0)
            else:
                value, way, column = plane(q, source), ACROSS, (q, source)
            if cy:
                edge = 0 if cy == 1 else length - 1
                k = where_is[way][column]
                far = packs(way)
                if (edge - k) % length:
                    far = pltpu.roll(far, (edge - k) % length, 1)
                value = jnp.where(lanes == edge, far, pltpu.roll(value, cy % length, 1))
            if cz:
                value = pltpu.roll(value, cz % depth, 0)
            store(q, x, value)


def collide(load, store, solid=None):
    density = None
    moment = [None, None, None]
    for q, velocity in enumerate(VELOCITY):
        value = load(q)
        density = value if density is None else density + value
        for axis in range(3):
            if velocity[axis]:
                signed = value if velocity[axis] == 1 else -value
                moment[axis] = signed if moment[axis] is None else moment[axis] + signed
    flow = [m / density for m in moment]
    square = flow[0] * flow[0] + flow[1] * flow[1] + flow[2] * flow[2]
    base = 1.0 - 1.5 * square
    scaled = {w: (RELAXATION * w) * density for w in sorted(set(WEIGHT))}
    for q in range(14):
        along = None
        for axis in range(3):
            if VELOCITY[q][axis]:
                term = flow[axis] if VELOCITY[q][axis] == 1 else -flow[axis]
                along = term if along is None else along + term
        if along is None:
            pairs = [(q, scaled[WEIGHT[q]] * base)]
        else:
            even = scaled[WEIGHT[q]] * (base + 4.5 * along * along)
            odd = scaled[WEIGHT[q]] * (3.0 * along)
            pairs = [(q, even + odd), (26 - q, even - odd)]
        values = [load(p) for p, _ in pairs]
        for (p, equilibrium), value, other in zip(pairs, values, values[::-1]):
            relaxed = (1.0 - RELAXATION) * value + equilibrium
            if solid is not None:
                relaxed = jnp.where(solid, other, relaxed)
            store(p, relaxed)


def kernel(
    groups, layers, fringe_count, *refs,
):
    operands, outs, loaded, load_sem, *scratch = (
        refs[:8], refs[8:12], refs[12:20], *refs[20:]
    )
    loads = [
        pltpu.make_async_copy(a, b, load_sem.at[min(i, 4) if i < 7 else 5])
        for i, (a, b) in enumerate(zip(operands, loaded))
    ]
    for copy in loads:
        copy.start()
    steps(groups, layers, fringe_count, loads, load_sem, *loaded, *outs, *scratch)


def steps(
    groups, layers, fringe_count, loads, load_sem, donor, target, slot, fringe,
    bg, body, solid, weights, out_bg, rd_body, gain, state,
    bgx_send, bgx_recv, bdx_send, bdx_recv, pk_send, pk_recv,
    cur_bg, cur_body, rd_bg, contrib, outgoing, arrived,
    sum_send, sum_recv, interp, chosen, label, span, sent, landed,
):
    gx, gy = lax.axis_index("gx"), lax.axis_index("gy")
    devices = groups * layers
    me = gx * layers + gy
    jobs = weights.shape[0]
    depth, length = cur_body.shape[1], cur_body.shape[2]
    width = cur_bg.shape[1]
    right = lax.rem(gx + 1, groups)
    left = lax.rem(gx + groups - 1, groups)
    other = lax.rem(gy + 1, layers)
    peer = [(right, gy), (left, gy), (gx, other), (right, other), (left, other)]
    f32, bf16 = jnp.float32, jnp.bfloat16

    barrier = pltpu.get_barrier_semaphore()

    def greet(k, carry):
        d = lax.rem(me + k, devices)
        pl.semaphore_signal(
            barrier, inc=1, device_id=(lax.div(d, layers), lax.rem(d, layers)), device_id_type=MESH
        )
        return carry

    with jax.named_scope("greet"):
        unrolled(1, devices, greet)

    lanes = lax.broadcasted_iota(jnp.int32, (depth, length), 1)
    rows = lax.broadcasted_iota(jnp.int32, (depth, length), 0)
    message_rows = lax.broadcasted_iota(jnp.int32, (HALF, length), 0)
    bg_columns = column_lists(width)
    body_columns = column_lists(1)
    ways = (ACROSS, ACROSS_RIGHT, ACROSS_LEFT)
    bg_first = {w: 0 for w in ways}
    body_first = {w: len(bg_columns[w]) for w in ways}
    blank = jnp.zeros((depth, length), f32)

    counts = {"sent": 0}

    def size(ref):
        return int(np.prod(ref.shape)) * jnp.dtype(ref.dtype).itemsize

    def remote(src, dst, phase, to, times=1):
        for key in ("sent", phase):
            counts[key] = counts.get(key, 0) + times * size(src)
        return pltpu.make_async_remote_copy(
            src_ref=src, dst_ref=dst, send_sem=sent, recv_sem=landed.at[phase], device_id=to,
            device_id_type=MESH
        )

    def wait_all(key):
        part = span.at[pl.ds(0, counts[key] // (4 * length))]
        assert counts[key] == size(part)
        pltpu.make_async_copy(part, part, sent if key == "sent" else landed.at[key]).wait()

    def pack_copies(i, phases):
        return [
            remote(pk_send.at[i, w - 2], pk_recv.at[i, w - 2], phase, peer[w])
            for w, phase in zip(ways, phases)
        ]

    def x_copies(send, recv, step, planes, phase):
        return [
            remote(send.at[step, w, pl.ds(0, planes)], recv.at[step, w, pl.ds(0, planes)], phase, peer[w])
            for w in (RIGHT, LEFT)
        ]

    packs = [pack_copies(0, (0, 1, 1)), pack_copies(1, (2, 3, 3)), pack_copies(2, (5, 5, 5))]
    bg_x = [x_copies(bgx_send, bgx_recv, step, 10 - step, 1 + 2 * step) for step in range(STEPS)]
    body_x = [x_copies(bdx_send, bdx_recv, step, 9, 4 + step) for step in range(STEPS)]

    def pack_bg(w):
        return pack_columns(blank, lambda q, x: cur_bg[q, x], bg_columns[w], bg_first[w], lanes, length)

    def pack_body(packed, source, w):
        return pack_columns(packed, lambda q, x: source[q], body_columns[w], body_first[w], lanes, length)

    def prepare_bg_x(step):
        for k in range(9):
            bgx_send[step, RIGHT, k] = cur_bg[18 + k, width - 1].astype(bf16)
            bgx_send[step, LEFT, k] = cur_bg[k, 0].astype(bf16)

    def prepare_body_x(step, source):
        for k in range(9):
            bdx_send[step, RIGHT, k] = source[18 + k].astype(bf16)
            bdx_send[step, LEFT, k] = source[k].astype(bf16)

    def stream_bg(step, inner, outer):
        def store(q, x, value):
            p = q if x == 0 else 26 - q
            rd_bg[pl.ds((p * width + x) * depth, depth), :] = value

        stream(
            lambda q, x: cur_bg[q, x],
            lambda w, k: bgx_recv[step, w, k].astype(f32),
            lambda w: pk_recv[step, w - 2].astype(f32),
            bg_first, width, lanes, depth, length, store, inner, outer,
        )

    def stream_body(step):
        source = body if step == 0 else cur_body

        def store(q, x, value):
            rd_body[q] = value

        stream(
            lambda q, x: source[q],
            lambda w, k: bdx_recv[step, w, k].astype(f32),
            lambda w: pk_recv[2 * step, w - 2].astype(f32),
            body_first, 1, lanes, depth, length, store,
        )

    def collide_bg(last):
        for x in range(width):
            def load(q):
                p = q if x == 0 else 26 - q
                return rd_bg[pl.ds((p * width + x) * depth, depth), :]

            def store(q, value):
                if last:
                    out_bg[q, pl.ds(x, depth, stride=width), :] = value
                else:
                    cur_bg[q, x] = value

            collide(load, store)

    group = next(g for g in (16, 8, 4, 2, 1) if jobs % g == 0)

    def contributions(part):
        start = part * EARLY

        def some(i, total):
            for k in range(group):
                j = i * group + k
                d = donor[j]
                first = (start * width + lax.rem(d, width)) * depth + lax.div(d, width)
                picked = rd_bg[pl.ds(first, HALF, stride=width * depth), :]
                product = jnp.dot(picked.astype(bf16), weights[j], preferred_element_type=f32)
                contrib[part, j] = product
                total = total + product
            return total

        total = lax.fori_loop(0, jobs // group, some, jnp.zeros((HALF, length), f32))
        if part == 0:
            total = jnp.where(message_rows < EARLY, total, 0.0)
        return jnp.sum(total, axis=0, keepdims=True)

    def message(part, d, c):
        value = contrib[part, chosen[d * CAP + c]]
        entry = jnp.full((HALF, length), label[d * CAP + c], jnp.int32).astype(f32)
        return jnp.where(message_rows == EARLY, entry, value).astype(bf16)

    def send_contributions(step, part, count=True):
        phase = 6 + 2 * step + part
        counts[phase] = (groups - 1) * CAP * HALF * length * 2
        counts["sent"] += counts[phase] if count else 0

        def to(k, carry):
            d = lax.bitwise_xor(gx, groups - k) if groups & (groups - 1) == 0 else lax.rem(gx + k, groups)
            for c in range(CAP):
                outgoing[step, part, d, pl.ds(c * HALF, HALF), :] = message(part, d, c)
            start_one(outgoing.at[step, part, d], arrived.at[step, part, gx], phase, (d, gy))
            return carry

        unrolled(1, groups, to)
        for c in range(CAP):
            arrived[step, part, gx, pl.ds(c * HALF, HALF), :] = message(part, gx, c)

    def start_one(src, dst, phase, to):
        pltpu.make_async_remote_copy(
            src_ref=src, dst_ref=dst, send_sem=sent, recv_sem=landed.at[phase], device_id=to,
            device_id_type=MESH
        ).start()

    def send_sums(step, mass_target, mass_interp):
        both = jnp.concatenate([mass_target, mass_interp], axis=0)
        sum_send[step] = both
        sum_recv[step, me] = both
        phase = 10 + step
        counts[phase] = (devices - 1) * 2 * length * 4
        counts["sent"] += counts[phase]

        def to(k, carry):
            d = lax.rem(me + k, devices)
            start_one(sum_send.at[step], sum_recv.at[step, me], phase, (lax.div(d, layers), lax.rem(d, layers)))
            return carry

        unrolled(1, devices, to)

    with jax.named_scope("loads"):
        for copy in loads[:4]:
            copy.wait()
        part = span.at[pl.ds(0, (size(bg) + size(body) + size(solid)) // (4 * length))]
        pltpu.make_async_copy(part, part, load_sem.at[4]).wait()
    hits = [rows == fringe[r] for r in range(fringe_count)]
    covered = functools.reduce(jnp.logical_or, hits)

    def mass_ahead(source):
        ahead = {0: (mine, ACROSS), 1: (bgx_recv[0, LEFT, 9].astype(f32), ACROSS_LEFT),
                 -1: (bgx_recv[0, RIGHT, 9].astype(f32), ACROSS_RIGHT)}
        held = blank
        for q, (cx, cy, cz) in enumerate(VELOCITY):
            share, way = ahead[cx]
            if cy:
                far = pk_recv[0, way - 2].astype(f32)
                if cy == -1:
                    far = pltpu.roll(far, 1, 1)
                share = jnp.where(lanes == (length - 1 if cy == 1 else 0), far, share)
            if cz:
                share = pltpu.roll(share, (-cz) % depth, 0)
            held = held + share * source[q]
        return jnp.sum(held, axis=0, keepdims=True)

    def gather(step, part):
        wait_all(6 + 2 * step + part)
        many = next(n for n in (4, 2, 1) if groups % n == 0)

        def some(i, totals):
            for o in [i * many + k for k in range(many)]:
                for c in range(CAP):
                    value = arrived[step, part, o, pl.ds(c * HALF, HALF), :].astype(f32)
                    entry = value[EARLY : EARLY + 1]
                    totals = tuple(
                        t + jnp.where(entry == float(r), value, 0.0) for r, t in enumerate(totals)
                    )
            return totals

        zero = jnp.zeros((HALF, length), f32)
        totals = lax.fori_loop(0, groups // many, some, (zero,) * (2 * fringe_count))
        for r in range(2 * fringe_count):
            interp[part, r] = totals[r]

    def row(r, p):
        part = p >= EARLY
        p -= part * EARLY
        return interp[int(part), r, p : p + 1, :]

    def halve():
        for q in range(27):
            old = rd_body[q]
            fresh = jnp.zeros((depth, length), f32)
            for r in range(fringe_count):
                fresh = jnp.where(hits[r], row(r, q) + row(fringe_count + r, 26 - q), fresh)
            rd_body[q] = jnp.where(covered, 0.5 * old, old)
            gain[q] = 0.5 * fresh

    def ratio(step):
        wait_all(10 + step)
        sums = jnp.sum(jnp.sum(sum_recv[step], axis=0), axis=1, keepdims=True)
        return sums[0:1] / sums[1:2]

    def mixed(factor):
        return lambda q: jnp.where(covered, rd_body[q] + factor * gain[q], rd_body[q])

    with jax.named_scope("prep0"):
        for q in range(27):
            for x in range(width):
                cur_bg[q, x] = bg[q, pl.ds(x, depth, stride=width), :]
        mine = covered.astype(f32)
        prepare_bg_x(0)
        for w in ways:
            packed = pack_body(pack_bg(w), body, w)
            pk_send[0, w - 2] = jnp.where(lanes == length - 1, mine, packed).astype(bf16)
        prepare_body_x(0, body)
        for w in (RIGHT, LEFT):
            bgx_send[0, w, 9] = mine.astype(bf16)
        tail = (HALF + EARLY - 27) * width * depth
        rd_bg[pl.ds(27 * width * depth, tail), :] = jnp.zeros((tail, length), f32)
        for part in range(2):
            contrib[part, jobs] = jnp.zeros((HALF, length), f32)

    def choose(d, carry):
        def scan(i, found):
            first, second = found
            for k in range(group):
                j = jobs - 1 - (i * group + k)
                match = target[j] == d
                second = jnp.where(match, first, second)
                first = jnp.where(match, j, first)
            return first, second

        found = lax.fori_loop(0, jobs // group, scan, (jnp.int32(jobs), jnp.int32(jobs)))
        for c in range(CAP):
            chosen[d * CAP + c] = found[c]
            j = jnp.minimum(found[c], jobs - 1)
            held = slot[j] + fringe_count * lax.rem(donor[j], width)
            label[d * CAP + c] = jnp.where(found[c] < jobs, held, -1)
        return carry

    is_solid = solid[...] == 1

    def store_body(q, value):
        cur_body[q] = value

    with jax.named_scope("barrier"):
        pl.semaphore_wait(barrier, devices - 1)
    with jax.named_scope("start_halo0"):
        for copy in packs[0][:1] + bg_x[0] + packs[0][1:]:
            copy.start()
    with jax.named_scope("choose"):
        lax.fori_loop(0, groups, choose, 0)
    with jax.named_scope("across0"):
        wait_all(0)
    with jax.named_scope("inner0"):
        stream_bg(0, True, False)
    with jax.named_scope("load7"):
        loads[7].wait()
    with jax.named_scope("early0"):
        first_interp = contributions(0)
    with jax.named_scope("send_early0"):
        send_contributions(0, 0)
    with jax.named_scope("start_body0"):
        for copy in body_x[0]:
            copy.start()
    with jax.named_scope("halo0"):
        wait_all(1)
    with jax.named_scope("outer0"):
        stream_bg(0, False, True)
    with jax.named_scope("collide0"):
        collide_bg(False)
    with jax.named_scope("prepare1"):
        prepare_bg_x(1)
        for copy in bg_x[1]:
            copy.start()
        for w in ways:
            pk_send[1, w - 2] = pack_bg(w).astype(bf16)
        for copy in packs[1]:
            copy.start()
    with jax.named_scope("late0"):
        mass_interp = first_interp + contributions(1)
    with jax.named_scope("sums0"):
        send_sums(0, mass_ahead(body), mass_interp)
    with jax.named_scope("send_late0"):
        send_contributions(0, 1)
    with jax.named_scope("across1"):
        wait_all(2)
    with jax.named_scope("inner1"):
        stream_bg(1, True, False)
    with jax.named_scope("early1"):
        first_interp = contributions(0)
    with jax.named_scope("send_early1b"):
        @pl.when(gx >= groups // 2)
        def _():
            send_contributions(1, 0, False)

    with jax.named_scope("gather_early0"):
        gather(0, 0)
    with jax.named_scope("halo1"):
        wait_all(3)
    with jax.named_scope("send_early1"):
        @pl.when(gx < groups // 2)
        def _():
            send_contributions(1, 0, True)

    with jax.named_scope("outer1"):
        stream_bg(1, False, True)
    with jax.named_scope("late1"):
        mass_interp = first_interp + contributions(1)
    with jax.named_scope("send_late1"):
        send_contributions(1, 1)
    with jax.named_scope("body_halo0"):
        wait_all(4)
    with jax.named_scope("body0"):
        stream_body(0)
    with jax.named_scope("gather_late0"):
        gather(0, 1)
    with jax.named_scope("halve0"):
        halve()
    with jax.named_scope("ratio0"):
        factor = ratio(0)
    with jax.named_scope("collide_body0"):
        collide(mixed(factor), store_body, is_solid)
    with jax.named_scope("prepare_body1"):
        prepare_body_x(1, cur_body)
        for copy in body_x[1]:
            copy.start()
        for w in ways:
            pk_send[2, w - 2] = pack_body(blank, cur_body, w).astype(bf16)
        for copy in packs[2]:
            copy.start()
    with jax.named_scope("sums1"):
        send_sums(1, mass_ahead(cur_body), mass_interp)
    with jax.named_scope("collide1"):
        collide_bg(True)
    with jax.named_scope("gather_early1"):
        gather(1, 0)
    with jax.named_scope("gather_late1"):
        gather(1, 1)
    with jax.named_scope("body_halo1"):
        wait_all(5)
    with jax.named_scope("body1"):
        stream_body(1)
    with jax.named_scope("halve1"):
        halve()
    with jax.named_scope("ratio1"):
        state[1] = mine
        state[2] = is_solid.astype(f32)
        state[0] = jnp.broadcast_to(ratio(1), (depth, length))
    with jax.named_scope("drain"):
        wait_all("sent")


def finish(bg, body, gain, state, out_bg, out_body, done, sems):
    stores = [
        pltpu.make_async_copy(a, b, sems.at[i]) for i, (a, b) in enumerate(((bg, out_bg), (done, out_body)))
    ]
    stores[0].start()
    factor, covered, solid = state[0], state[1] > 0.5, state[2] > 0.5

    def store(q, value):
        done[q] = value

    collide(lambda q: jnp.where(covered, body[q] + factor * gain[q], body[q]), store, solid)
    stores[1].start()
    for copy in stores:
        copy.wait()


def local(groups, layers, background, overset_block, solid_mask, donor_tile, target_rank,
          target_slot, fringe_tiles, interp_weights):
    _, depth, width, length = background.shape
    jobs, nodes = interp_weights.shape[2], interp_weights.shape[3]
    assert overset_block.shape[2] == 1 and width == 2 and nodes == length and layers == 2 and STEPS == 2
    fringe_count = fringe_tiles.shape[-1]
    devices = groups * layers
    plane = (depth, length)
    f32, bf16 = jnp.float32, jnp.bfloat16
    vmem, smem = pltpu.VMEM, pltpu.SMEM
    dma = pltpu.SemaphoreType.DMA
    span_rows = STEPS * (2 * groups * CAP * HALF + 2 * devices + 64 * depth)
    held = pl.pallas_call(
        functools.partial(kernel, groups, layers, fringe_count),
        out_shape=(
            vmem((27, depth * width, length), f32),
            vmem((27,) + plane, f32),
            vmem((27,) + plane, f32),
            vmem((3,) + plane, f32),
        ),
        in_specs=[pl.BlockSpec(memory_space=pltpu.HBM)] * 8,
        out_specs=(pl.BlockSpec(memory_space=pltpu.VMEM),) * 4,
        scratch_shapes=[
            smem((jobs,), jnp.int32),
            smem((jobs,), jnp.int32),
            smem((jobs,), jnp.int32),
            smem((fringe_count,), jnp.int32),
            vmem((27, depth * width, length), f32),
            vmem((27, depth, length), f32),
            vmem((depth, length), jnp.int32),
            vmem((jobs, nodes, nodes), bf16),
            dma((6,)),
            vmem((STEPS, 2, 10) + plane, bf16),
            vmem((STEPS, 2, 10) + plane, bf16),
            vmem((STEPS, 2, 9) + plane, bf16),
            vmem((STEPS, 2, 9) + plane, bf16),
            vmem((3, 3) + plane, bf16),
            vmem((3, 3) + plane, bf16),
            vmem((27, width) + plane, f32),
            vmem((27,) + plane, f32),
            vmem(((HALF + EARLY) * width * depth, length), f32),
            vmem((2, jobs + 1, HALF, length), f32),
            vmem((STEPS, 2, groups, CAP * HALF, length), bf16),
            vmem((STEPS, 2, groups, CAP * HALF, length), bf16),
            vmem((STEPS, 2, length), f32),
            vmem((STEPS, devices, 2, length), f32),
            vmem((2, 2 * fringe_count, HALF, length), f32),
            smem((groups * CAP,), jnp.int32),
            smem((groups * CAP,), jnp.int32),
            vmem((span_rows, length), f32),
            dma(()),
            dma((12,)),
        ],
        compiler_params=pltpu.CompilerParams(
            collective_id=0, has_side_effects=True, vmem_limit_bytes=48000000
        ),
    )(*(pltpu.with_memory_space_constraint(a, pltpu.HBM) for a in (
        donor_tile.reshape(jobs),
        target_rank.reshape(jobs),
        target_slot.reshape(jobs),
        fringe_tiles.reshape(fringe_count),
        background.reshape(27, depth * width, length),
        overset_block.reshape(27, depth, length),
        solid_mask.reshape(depth, length),
        interp_weights.reshape(jobs, nodes, nodes),
    )))
    next_bg, next_body = pl.pallas_call(
        finish,
        out_shape=(
            jax.ShapeDtypeStruct((27, depth * width, length), f32),
            jax.ShapeDtypeStruct((27, depth, length), f32),
        ),
        in_specs=[pl.BlockSpec(memory_space=pltpu.VMEM)] * 4,
        out_specs=(pl.BlockSpec(memory_space=pltpu.HBM),) * 2,
        scratch_shapes=[vmem((27,) + plane, f32), dma((2,))],
    )(*(pltpu.with_memory_space_constraint(a, pltpu.VMEM) for a in held))
    return next_bg.reshape(background.shape), next_body.reshape(overset_block.shape)


def solution(mesh):
    return jax.shard_map(
        functools.partial(local, mesh.shape["gx"], mesh.shape["gy"]),
        mesh=mesh,
        in_specs=(
            P(None, None, "gx", "gy"),
            P(None, None, "gx", "gy"),
            P(None, "gx", "gy"),
            P("gx", "gy", None),
            P("gx", "gy", None, None),
            P("gx", "gy", None),
            P("gx", "gy", None),
            P("gx", "gy", None, None, None),
        ),
        out_specs=(P(None, None, "gx", "gy"), P(None, None, "gx", "gy")),
        check_vma=False,
    )
```

```python
import functools

import jax
import jax.numpy as jnp
import numpy as np
from jax import lax
from jax.experimental import pallas as pl
from jax.experimental.pallas import tpu as pltpu
from jax.sharding import PartitionSpec as P

CAP = 2
STEPS = 2
RELAXATION = 1.25
HALF = 16
EARLY = 15
MESH = pl.DeviceIdType.MESH

VELOCITY = [(x, y, z) for x in (-1, 0, 1) for y in (-1, 0, 1) for z in (-1, 0, 1)]
WEIGHT = [(8 / 27, 2 / 27, 1 / 54, 1 / 216)[abs(x) + abs(y) + abs(z)] for x, y, z in VELOCITY]

RIGHT, LEFT, ACROSS, ACROSS_RIGHT, ACROSS_LEFT = range(5)


def column_lists(width):
    lists = {ACROSS: [], ACROSS_RIGHT: [], ACROSS_LEFT: []}
    for q, (cx, cy, _) in enumerate(VELOCITY):
        if cy == 0:
            continue
        for x in range(width):
            to = x + cx
            way = ACROSS_RIGHT if to >= width else ACROSS_LEFT if to < 0 else ACROSS
            lists[way].append((q, x))
    return lists


def unrolled(start, stop, body):
    step = next(n for n in (16, 8, 4, 2, 1) if (stop - start) // n >= 1)

    def several(i, carry):
        for k in range(step):
            body(start + i * step + k, 0)
        return carry

    whole = (stop - start) // step
    lax.fori_loop(0, whole, several, 0)
    for k in range(start + whole * step, stop):
        body(k, 0)


def pack_columns(packed, plane, columns, first, lanes, length):
    for k, (q, x) in enumerate(columns, first):
        edge = length - 1 if VELOCITY[q][1] == 1 else 0
        value = plane(q, x)
        if (k - edge) % length:
            value = pltpu.roll(value, (k - edge) % length, 1)
        packed = jnp.where(lanes == k, value, packed)
    return packed


def stream(plane, across_x, packs, first, width, lanes, depth, length, store, inner=True, outer=True):
    lists = column_lists(width)
    where_is = {way: {c: k for k, c in enumerate(cols, first[way])} for way, cols in lists.items()}
    for q, (cx, cy, cz) in enumerate(VELOCITY):
        for x in range(width):
            source = x - cx
            if not (inner if 0 <= source < width else outer):
                continue
            if source < 0:
                value, way, column = across_x(RIGHT, q - 18), ACROSS_RIGHT, (q, width - 1)
            elif source >= width:
                value, way, column = across_x(LEFT, q), ACROSS_LEFT, (q, 0)
            else:
                value, way, column = plane(q, source), ACROSS, (q, source)
            if cy:
                edge = 0 if cy == 1 else length - 1
                k = where_is[way][column]
                far = packs(way)
                if (edge - k) % length:
                    far = pltpu.roll(far, (edge - k) % length, 1)
                value = jnp.where(lanes == edge, far, pltpu.roll(value, cy % length, 1))
            if cz:
                value = pltpu.roll(value, cz % depth, 0)
            store(q, x, value)


def collide(load, store, solid=None):
    density = None
    moment = [None, None, None]
    for q, velocity in enumerate(VELOCITY):
        value = load(q)
        density = value if density is None else density + value
        for axis in range(3):
            if velocity[axis]:
                signed = value if velocity[axis] == 1 else -value
                moment[axis] = signed if moment[axis] is None else moment[axis] + signed
    flow = [m / density for m in moment]
    square = flow[0] * flow[0] + flow[1] * flow[1] + flow[2] * flow[2]
    base = 1.0 - 1.5 * square
    scaled = {w: (RELAXATION * w) * density for w in sorted(set(WEIGHT))}
    for q in range(14):
        along = None
        for axis in range(3):
            if VELOCITY[q][axis]:
                term = flow[axis] if VELOCITY[q][axis] == 1 else -flow[axis]
                along = term if along is None else along + term
        if along is None:
            pairs = [(q, scaled[WEIGHT[q]] * base)]
        else:
            even = scaled[WEIGHT[q]] * (base + 4.5 * along * along)
            odd = scaled[WEIGHT[q]] * (3.0 * along)
            pairs = [(q, even + odd), (26 - q, even - odd)]
        values = [load(p) for p, _ in pairs]
        for (p, equilibrium), value, other in zip(pairs, values, values[::-1]):
            relaxed = (1.0 - RELAXATION) * value + equilibrium
            if solid is not None:
                relaxed = jnp.where(solid, other, relaxed)
            store(p, relaxed)


def kernel(
    groups, layers, fringe_count, *refs,
):
    operands, outs, loaded, load_sem, *scratch = (
        refs[:8], refs[8:12], refs[12:20], *refs[20:]
    )
    loads = [
        pltpu.make_async_copy(a, b, load_sem.at[min(i, 4) if i < 7 else 5])
        for i, (a, b) in enumerate(zip(operands, loaded))
    ]
    for copy in loads:
        copy.start()
    steps(groups, layers, fringe_count, loads, load_sem, *loaded, *outs, *scratch)


def steps(
    groups, layers, fringe_count, loads, load_sem, donor, target, slot, fringe,
    bg, body, solid, weights, out_bg, rd_body, gain, state,
    bgx_send, bgx_recv, bdx_send, bdx_recv, pk_send, pk_recv,
    cur_bg, cur_body, rd_bg, contrib, outgoing, arrived,
    sum_send, sum_recv, interp, picks, chosen, label, span, sent, landed,
):
    gx, gy = lax.axis_index("gx"), lax.axis_index("gy")
    devices = groups * layers
    me = gx * layers + gy
    jobs = weights.shape[0]
    depth, length = cur_body.shape[1], cur_body.shape[2]
    width = cur_bg.shape[1]
    pitch = rd_bg.shape[0] // (HALF + EARLY)
    right = lax.rem(gx + 1, groups)
    left = lax.rem(gx + groups - 1, groups)
    other = lax.rem(gy + 1, layers)
    peer = [(right, gy), (left, gy), (gx, other), (right, other), (left, other)]
    f32, bf16 = jnp.float32, jnp.bfloat16

    barrier = pltpu.get_barrier_semaphore()

    def greet(k, carry):
        d = lax.rem(me + k, devices)
        pl.semaphore_signal(
            barrier, inc=1, device_id=(lax.div(d, layers), lax.rem(d, layers)), device_id_type=MESH
        )
        return carry

    with jax.named_scope("greet"):
        unrolled(1, devices, greet)

    lanes = lax.broadcasted_iota(jnp.int32, (depth, length), 1)
    rows = lax.broadcasted_iota(jnp.int32, (depth, length), 0)
    message_rows = lax.broadcasted_iota(jnp.int32, (HALF, length), 0)
    bg_columns = column_lists(width)
    body_columns = column_lists(1)
    ways = (ACROSS, ACROSS_RIGHT, ACROSS_LEFT)
    bg_first = {w: 0 for w in ways}
    body_first = {w: len(bg_columns[w]) for w in ways}
    blank = jnp.zeros((depth, length), f32)

    counts = {"sent": 0}

    def size(ref):
        return int(np.prod(ref.shape)) * jnp.dtype(ref.dtype).itemsize

    def remote(src, dst, phase, to, times=1):
        for key in ("sent", phase):
            counts[key] = counts.get(key, 0) + times * size(src)
        return pltpu.make_async_remote_copy(
            src_ref=src, dst_ref=dst, send_sem=sent, recv_sem=landed.at[phase], device_id=to,
            device_id_type=MESH
        )

    def wait_all(key):
        part = span.at[pl.ds(0, counts[key] // (4 * length))]
        assert counts[key] == size(part)
        pltpu.make_async_copy(part, part, sent if key == "sent" else landed.at[key]).wait()

    def pack_copies(i, phases):
        return [
            remote(pk_send.at[i, w - 2], pk_recv.at[i, w - 2], phase, peer[w])
            for w, phase in zip(ways, phases)
        ]

    def x_copies(send, recv, step, planes, phase):
        return [
            remote(send.at[step, w, pl.ds(0, planes)], recv.at[step, w, pl.ds(0, planes)], phase, peer[w])
            for w in (RIGHT, LEFT)
        ]

    packs = [pack_copies(0, (0, 1, 1)), pack_copies(1, (2, 3, 3)), pack_copies(2, (5, 5, 5))]
    bg_x = [x_copies(bgx_send, bgx_recv, step, 10 - step, 1 + 2 * step) for step in range(STEPS)]
    body_x = [x_copies(bdx_send, bdx_recv, step, 9, 4 + step) for step in range(STEPS)]

    def pack_bg(w):
        return pack_columns(blank, lambda q, x: cur_bg[q, x], bg_columns[w], bg_first[w], lanes, length)

    def pack_body(packed, source, w):
        return pack_columns(packed, lambda q, x: source[q], body_columns[w], body_first[w], lanes, length)

    def prepare_bg_x(step):
        for k in range(9):
            bgx_send[step, RIGHT, k] = cur_bg[18 + k, width - 1].astype(bf16)
            bgx_send[step, LEFT, k] = cur_bg[k, 0].astype(bf16)

    def prepare_body_x(step, source):
        for k in range(9):
            bdx_send[step, RIGHT, k] = source[18 + k].astype(bf16)
            bdx_send[step, LEFT, k] = source[k].astype(bf16)

    def stream_bg(step, inner, outer):
        def store(q, x, value):
            p = q if x == 0 else 26 - q
            rd_bg[pl.ds(p * pitch + x * depth, depth), :] = value

        stream(
            lambda q, x: cur_bg[q, x],
            lambda w, k: bgx_recv[step, w, k].astype(f32),
            lambda w: pk_recv[step, w - 2].astype(f32),
            bg_first, width, lanes, depth, length, store, inner, outer,
        )

    def stream_body(step):
        source = body if step == 0 else cur_body

        def store(q, x, value):
            rd_body[q] = value

        stream(
            lambda q, x: source[q],
            lambda w, k: bdx_recv[step, w, k].astype(f32),
            lambda w: pk_recv[2 * step, w - 2].astype(f32),
            body_first, 1, lanes, depth, length, store,
        )

    def collide_bg(last):
        for x in range(width):
            def load(q):
                p = q if x == 0 else 26 - q
                return rd_bg[pl.ds(p * pitch + x * depth, depth), :]

            def store(q, value):
                if last:
                    out_bg[q, pl.ds(x, depth, stride=width), :] = value
                else:
                    cur_bg[q, x] = value

            collide(load, store)

    group = next(g for g in (16, 8, 4, 2, 1) if jobs % g == 0)

    def contributions(part):
        start = part * EARLY

        def some(i, total):
            for k in range(group):
                j = i * group + k
                d = donor[j]
                first = start * pitch + lax.rem(d, width) * depth + lax.div(d, width)
                picked = rd_bg[pl.ds(first, HALF, stride=pitch), :]
                product = jnp.dot(picked.astype(bf16), weights[j], preferred_element_type=f32)
                contrib[part, j] = product
                total = total + product
            return total

        total = lax.fori_loop(0, jobs // group, some, jnp.zeros((HALF, length), f32))
        if part == 0:
            total = jnp.where(message_rows < EARLY, total, 0.0)
        return jnp.sum(total, axis=0, keepdims=True)

    def message(part, d, c):
        value = contrib[part, chosen[d * CAP + c]]
        entry = jnp.full((HALF, length), label[d * CAP + c], jnp.int32).astype(f32)
        return jnp.where(message_rows == EARLY, entry, value).astype(bf16)

    def send_contributions(step, part, count=True):
        phase = 6 + 2 * step + part
        counts[phase] = (groups - 1) * CAP * HALF * length * 2
        counts["sent"] += counts[phase] if count else 0

        def to(k, carry):
            d = lax.bitwise_xor(gx, groups - k) if groups & (groups - 1) == 0 else lax.rem(gx + k, groups)
            for c in range(CAP):
                outgoing[step, part, d, pl.ds(c * HALF, HALF), :] = message(part, d, c)
            start_one(outgoing.at[step, part, d], arrived.at[step, part, gx], phase, (d, gy))
            return carry

        unrolled(1, groups, to)
        for c in range(CAP):
            arrived[step, part, gx, pl.ds(c * HALF, HALF), :] = message(part, gx, c)

    def start_one(src, dst, phase, to):
        pltpu.make_async_remote_copy(
            src_ref=src, dst_ref=dst, send_sem=sent, recv_sem=landed.at[phase], device_id=to,
            device_id_type=MESH
        ).start()

    def send_sums(step, mass_target, mass_interp):
        both = jnp.concatenate([mass_target, mass_interp], axis=0)
        sum_send[step] = both
        sum_recv[step, me] = both
        phase = 10 + step
        counts[phase] = (devices - 1) * 2 * length * 4
        counts["sent"] += counts[phase]

        def to(k, carry):
            d = lax.rem(me + k, devices)
            start_one(sum_send.at[step], sum_recv.at[step, me], phase, (lax.div(d, layers), lax.rem(d, layers)))
            return carry

        unrolled(1, devices, to)

    with jax.named_scope("loads"):
        for copy in loads[:4]:
            copy.wait()
        part = span.at[pl.ds(0, (size(bg) + size(body) + size(solid)) // (4 * length))]
        pltpu.make_async_copy(part, part, load_sem.at[4]).wait()
    hits = [rows == fringe[r] for r in range(fringe_count)]
    covered = functools.reduce(jnp.logical_or, hits)

    def mass_ahead(source):
        ahead = {0: (mine, ACROSS), 1: (bgx_recv[0, LEFT, 9].astype(f32), ACROSS_LEFT),
                 -1: (bgx_recv[0, RIGHT, 9].astype(f32), ACROSS_RIGHT)}
        held = blank
        for q, (cx, cy, cz) in enumerate(VELOCITY):
            share, way = ahead[cx]
            if cy:
                far = pk_recv[0, way - 2].astype(f32)
                if cy == -1:
                    far = pltpu.roll(far, 1, 1)
                share = jnp.where(lanes == (length - 1 if cy == 1 else 0), far, share)
            if cz:
                share = pltpu.roll(share, (-cz) % depth, 0)
            held = held + share * source[q]
        return jnp.sum(held, axis=0, keepdims=True)

    chunk, deep = picks.shape[0], picks.shape[2]
    chunk = groups // chunk

    def prepare_picks():
        tall = picks.shape[1]
        at_row = lax.broadcasted_iota(jnp.int32, (tall, length), 0)
        at_lane = lax.broadcasted_iota(jnp.int32, (tall, length), 1)
        diagonal = lax.rem(at_row, HALF) == lax.rem(at_lane, HALF)
        row_class = lax.div(at_row, HALF).astype(f32)
        lane_entry = lax.div(lax.broadcasted_iota(jnp.int32, (1, length), 1), HALF)

        def one(i, carry):
            for t in range(deep // length):
                classes = jnp.full((1, length), -1.0, f32)
                for e in range(length // HALF):
                    o, c = i * chunk + (t * (length // HALF) + e) // CAP, e % CAP
                    entry = arrived[0, 0, o, pl.ds(c * HALF, HALF), :].astype(f32)[EARLY : EARLY + 1]
                    classes = jnp.where(lane_entry == e, entry, classes)
                hit = jnp.logical_and(diagonal, row_class == classes)
                picks[i, :, pl.ds(t * length, length)] = jnp.where(hit, 1.0, 0.0).astype(bf16)
            return carry

        lax.fori_loop(0, groups // chunk, one, 0)

    def gather(step, part):
        wait_all(6 + 2 * step + part)
        if step == 0 and part == 0:
            prepare_picks()

        def some(i, total):
            block = arrived[step, part, pl.ds(i * chunk, chunk)].reshape(deep, length)
            return total + jnp.dot(picks[i], block, preferred_element_type=f32)

        total = jnp.zeros((picks.shape[1], length), f32)
        total = some(0, total) if groups == chunk else lax.fori_loop(0, groups // chunk, some, total)
        interp[part] = total.reshape(interp.shape[1:])

    def row(r, p):
        part = p >= EARLY
        p -= part * EARLY
        return interp[int(part), r, p : p + 1, :]

    def halve():
        for q in range(27):
            old = rd_body[q]
            fresh = jnp.zeros((depth, length), f32)
            for r in range(fringe_count):
                fresh = jnp.where(hits[r], row(r, q) + row(fringe_count + r, 26 - q), fresh)
            rd_body[q] = jnp.where(covered, 0.5 * old, old)
            gain[q] = 0.5 * fresh

    def ratio(step):
        wait_all(10 + step)
        sums = jnp.sum(jnp.sum(sum_recv[step], axis=0), axis=1, keepdims=True)
        return sums[0:1] / sums[1:2]

    def mixed(factor):
        return lambda q: jnp.where(covered, rd_body[q] + factor * gain[q], rd_body[q])

    with jax.named_scope("prep0"):
        for q in range(27):
            for x in range(width):
                cur_bg[q, x] = bg[q, pl.ds(x, depth, stride=width), :]
        mine = covered.astype(f32)
        prepare_bg_x(0)
        for w in ways:
            packed = pack_body(pack_bg(w), body, w)
            pk_send[0, w - 2] = jnp.where(lanes == length - 1, mine, packed).astype(bf16)
        prepare_body_x(0, body)
        for w in (RIGHT, LEFT):
            bgx_send[0, w, 9] = mine.astype(bf16)
        tail = (HALF + EARLY - 27) * pitch
        rd_bg[pl.ds(27 * pitch, tail), :] = jnp.zeros((tail, length), f32)
        for part in range(2):
            contrib[part, jobs] = jnp.zeros((HALF, length), f32)

    def choose(d, carry):
        def scan(i, found):
            first, second = found
            for k in range(group):
                j = jobs - 1 - (i * group + k)
                match = target[j] == d
                second = jnp.where(match, first, second)
                first = jnp.where(match, j, first)
            return first, second

        found = lax.fori_loop(0, jobs // group, scan, (jnp.int32(jobs), jnp.int32(jobs)))
        for c in range(CAP):
            chosen[d * CAP + c] = found[c]
            j = jnp.minimum(found[c], jobs - 1)
            held = slot[j] + fringe_count * lax.rem(donor[j], width)
            label[d * CAP + c] = jnp.where(found[c] < jobs, held, -1)
        return carry

    is_solid = solid[...] == 1

    def store_body(q, value):
        cur_body[q] = value

    with jax.named_scope("barrier"):
        pl.semaphore_wait(barrier, devices - 1)
    with jax.named_scope("start_halo0"):
        for copy in packs[0][:1] + bg_x[0] + packs[0][1:]:
            copy.start()
    with jax.named_scope("choose"):
        lax.fori_loop(0, groups, choose, 0)
    with jax.named_scope("across0"):
        wait_all(0)
    with jax.named_scope("inner0"):
        stream_bg(0, True, False)
    with jax.named_scope("load7"):
        loads[7].wait()
    with jax.named_scope("early0"):
        first_interp = contributions(0)
    with jax.named_scope("send_early0"):
        send_contributions(0, 0)
    with jax.named_scope("start_body0"):
        for copy in body_x[0]:
            copy.start()
    with jax.named_scope("halo0"):
        wait_all(1)
    with jax.named_scope("outer0"):
        stream_bg(0, False, True)
    with jax.named_scope("collide0"):
        collide_bg(False)
    with jax.named_scope("prepare1"):
        prepare_bg_x(1)
        for copy in bg_x[1]:
            copy.start()
        for w in ways:
            pk_send[1, w - 2] = pack_bg(w).astype(bf16)
        for copy in packs[1]:
            copy.start()
    with jax.named_scope("late0"):
        mass_interp = first_interp + contributions(1)
    with jax.named_scope("sums0"):
        send_sums(0, mass_ahead(body), mass_interp)
    with jax.named_scope("send_late0"):
        send_contributions(0, 1)
    with jax.named_scope("across1"):
        wait_all(2)
    with jax.named_scope("inner1"):
        stream_bg(1, True, False)
    with jax.named_scope("early1"):
        first_interp = contributions(0)
    with jax.named_scope("send_early1b"):
        @pl.when(gx >= groups // 2)
        def _():
            send_contributions(1, 0, False)

    with jax.named_scope("gather_early0"):
        gather(0, 0)
    with jax.named_scope("halo1"):
        wait_all(3)
    with jax.named_scope("send_early1"):
        @pl.when(gx < groups // 2)
        def _():
            send_contributions(1, 0, True)

    with jax.named_scope("outer1"):
        stream_bg(1, False, True)
    with jax.named_scope("late1"):
        mass_interp = first_interp + contributions(1)
    with jax.named_scope("send_late1"):
        send_contributions(1, 1)
    with jax.named_scope("body_halo0"):
        wait_all(4)
    with jax.named_scope("body0"):
        stream_body(0)
    with jax.named_scope("gather_late0"):
        gather(0, 1)
    with jax.named_scope("halve0"):
        halve()
    with jax.named_scope("ratio0"):
        factor = ratio(0)
    with jax.named_scope("collide_body0"):
        collide(mixed(factor), store_body, is_solid)
    with jax.named_scope("prepare_body1"):
        prepare_body_x(1, cur_body)
        for copy in body_x[1]:
            copy.start()
        for w in ways:
            pk_send[2, w - 2] = pack_body(blank, cur_body, w).astype(bf16)
        for copy in packs[2]:
            copy.start()
    with jax.named_scope("sums1"):
        send_sums(1, mass_ahead(cur_body), mass_interp)
    with jax.named_scope("collide1"):
        collide_bg(True)
    with jax.named_scope("gather_early1"):
        gather(1, 0)
    with jax.named_scope("gather_late1"):
        gather(1, 1)
    with jax.named_scope("body_halo1"):
        wait_all(5)
    with jax.named_scope("body1"):
        stream_body(1)
    with jax.named_scope("halve1"):
        halve()
    with jax.named_scope("ratio1"):
        state[1] = mine
        state[2] = is_solid.astype(f32)
        state[0] = jnp.broadcast_to(ratio(1), (depth, length))
    with jax.named_scope("drain"):
        wait_all("sent")


def finish(bg, body, gain, state, out_bg, out_body, done, sems):
    stores = [
        pltpu.make_async_copy(a, b, sems.at[i]) for i, (a, b) in enumerate(((bg, out_bg), (done, out_body)))
    ]
    stores[0].start()
    factor, covered, solid = state[0], state[1] > 0.5, state[2] > 0.5

    def store(q, value):
        done[q] = value

    collide(lambda q: jnp.where(covered, body[q] + factor * gain[q], body[q]), store, solid)
    stores[1].start()
    for copy in stores:
        copy.wait()


def local(groups, layers, background, overset_block, solid_mask, donor_tile, target_rank,
          target_slot, fringe_tiles, interp_weights):
    _, depth, width, length = background.shape
    jobs, nodes = interp_weights.shape[2], interp_weights.shape[3]
    assert overset_block.shape[2] == 1 and width == 2 and nodes == length and layers == 2 and STEPS == 2
    fringe_count = fringe_tiles.shape[-1]
    devices = groups * layers
    plane = (depth, length)
    f32, bf16 = jnp.float32, jnp.bfloat16
    vmem, smem = pltpu.VMEM, pltpu.SMEM
    dma = pltpu.SemaphoreType.DMA
    span_rows = STEPS * (2 * groups * CAP * HALF + 2 * devices + 64 * depth)
    chunk = next(n for n in (16, 8, 4) if groups % n == 0)
    assert length % (CAP * HALF) == 0 and (chunk * CAP * HALF) % length == 0
    held = pl.pallas_call(
        functools.partial(kernel, groups, layers, fringe_count),
        out_shape=(
            vmem((27, depth * width, length), f32),
            vmem((27,) + plane, f32),
            vmem((27,) + plane, f32),
            vmem((3,) + plane, f32),
        ),
        in_specs=[pl.BlockSpec(memory_space=pltpu.HBM)] * 8,
        out_specs=(pl.BlockSpec(memory_space=pltpu.VMEM),) * 4,
        scratch_shapes=[
            smem((jobs,), jnp.int32),
            smem((jobs,), jnp.int32),
            smem((jobs,), jnp.int32),
            smem((fringe_count,), jnp.int32),
            vmem((27, depth * width, length), f32),
            vmem((27, depth, length), f32),
            vmem((depth, length), jnp.int32),
            vmem((jobs, nodes, nodes), bf16),
            dma((6,)),
            vmem((STEPS, 2, 10) + plane, bf16),
            vmem((STEPS, 2, 10) + plane, bf16),
            vmem((STEPS, 2, 9) + plane, bf16),
            vmem((STEPS, 2, 9) + plane, bf16),
            vmem((3, 3) + plane, bf16),
            vmem((3, 3) + plane, bf16),
            vmem((27, width) + plane, f32),
            vmem((27,) + plane, f32),
            vmem(((HALF + EARLY) * (width * depth + 8), length), f32),
            vmem((2, jobs + 1, HALF, length), f32),
            vmem((STEPS, 2, groups, CAP * HALF, length), bf16),
            vmem((STEPS, 2, groups, CAP * HALF, length), bf16),
            vmem((STEPS, 2, length), f32),
            vmem((STEPS, devices, 2, length), f32),
            vmem((2, 2 * fringe_count, HALF, length), f32),
            vmem((groups // chunk, 2 * fringe_count * HALF, chunk * CAP * HALF), bf16),
            smem((groups * CAP,), jnp.int32),
            smem((groups * CAP,), jnp.int32),
            vmem((span_rows, length), f32),
            dma(()),
            dma((12,)),
        ],
        compiler_params=pltpu.CompilerParams(
            collective_id=0, has_side_effects=True, vmem_limit_bytes=48000000
        ),
    )(*(pltpu.with_memory_space_constraint(a, pltpu.HBM) for a in (
        donor_tile.reshape(jobs),
        target_rank.reshape(jobs),
        target_slot.reshape(jobs),
        fringe_tiles.reshape(fringe_count),
        background.reshape(27, depth * width, length),
        overset_block.reshape(27, depth, length),
        solid_mask.reshape(depth, length),
        interp_weights.reshape(jobs, nodes, nodes),
    )))
    next_bg, next_body = pl.pallas_call(
        finish,
        out_shape=(
            jax.ShapeDtypeStruct((27, depth * width, length), f32),
            jax.ShapeDtypeStruct((27, depth, length), f32),
        ),
        in_specs=[pl.BlockSpec(memory_space=pltpu.VMEM)] * 4,
        out_specs=(pl.BlockSpec(memory_space=pltpu.HBM),) * 2,
        scratch_shapes=[vmem((27,) + plane, f32), dma((2,))],
    )(*(pltpu.with_memory_space_constraint(a, pltpu.VMEM) for a in held))
    return next_bg.reshape(background.shape), next_body.reshape(overset_block.shape)


def solution(mesh):
    return jax.shard_map(
        functools.partial(local, mesh.shape["gx"], mesh.shape["gy"]),
        mesh=mesh,
        in_specs=(
            P(None, None, "gx", "gy"),
            P(None, None, "gx", "gy"),
            P(None, "gx", "gy"),
            P("gx", "gy", None),
            P("gx", "gy", None, None),
            P("gx", "gy", None),
            P("gx", "gy", None),
            P("gx", "gy", None, None, None),
        ),
        out_specs=(P(None, None, "gx", "gy"), P(None, None, "gx", "gy")),
        check_vma=False,
    )
```
